128 devices in a mesh: grp: 4 (over y), dev: 32 (over z, x, core).
Axes of the slice: x: 4, y: 4, z: 4, core: 2. Of those that a mesh axis runs over, the one named last changes fastest.
Arguments:
- points: float32 [3, 65536], P(None, 'dev'), may hold values from 0 to 1
- omega: bfloat16 [65536, 256], P('dev'), may hold values from -0.0234375 to 0.0234375
- pivots: int32 [32, 256], replicated, may hold values from 0 to 2047, as said below
- ranks: int32 [32], replicated, may hold values from 128 to 256, as said below
- owners: int32 [16], replicated, may hold values from 0 to 3, as said below
Outputs:
- interp: float32 [65536, 256], P(('grp', 'dev'))
- parent_samples: float32 [4, 8, 512, 256], P('grp', None, 'dev')
The draws below stay inside these ranges and needn't reach their ends.
Inputs may be any that keep to these rules, and one draw needn't show every extreme that they name: The 256 pivots of a leaf are distinct. `ranks`: some leaf has exactly 256 skeleton rows in every draw. `owners`: no owner holds more than 8 parents, and some owner holds exactly 8.
All inputs are finite; a program needn't handle non-finite values.
Results may differ from the reference program's by a relative error of at most 0.0097.
Values may be sent and summed in bfloat16 or wider, within the bound.
A program may use at most 192 MiB of HBM per device.

```python
import math
import jax
import jax.numpy as jnp
from jax import lax

LEAF = 2048
S = 256
RMAX = 256
N = 65536
LEAVES = 32
OWNERS = 4
PARENTS = 16
SLOTS = 8


def draw_points(key, part):
    bands = math.gcd(LEAVES, 4)
    sectors = LEAVES // bands
    leaf_of = jnp.arange(N, dtype=jnp.int32) // LEAF
    band_of = (leaf_of // sectors).astype(jnp.float32)
    sector_of = (leaf_of % sectors).astype(jnp.float32)
    first_key, second_key, third_key = jax.random.split(jax.random.fold_in(key, 5), 3)
    along = jax.random.uniform(first_key, (N,), jnp.float32)
    across = jax.random.uniform(second_key, (N,), jnp.float32)
    spread = jax.random.bernoulli(third_key, 0.5, (N,))
    patch_height = -1.0 + 2.0 * (band_of + along) / bands
    patch_angle = 2.0 * jnp.pi * (sector_of + across) / sectors
    free_height = -1.0 + 2.0 * along
    free_angle = 2.0 * jnp.pi * across
    height = jnp.where(spread, free_height, patch_height)
    angle = jnp.where(spread, free_angle, patch_angle)
    radial = jnp.sqrt(jnp.maximum(1.0 - height * height, 0.0))
    coord_x = 0.5 + 0.45 * radial * jnp.cos(angle)
    coord_y = 0.5 + 0.45 * radial * jnp.sin(angle)
    coord_z = 0.5 + 0.45 * height
    return jnp.stack([coord_x, coord_y, coord_z], axis=0).astype(jnp.float32)


def draw_pivots(key, part):
    leaf_keys = jax.random.split(jax.random.fold_in(key, 11), LEAVES)
    picks = jax.vmap(lambda one_key: jax.random.permutation(one_key, LEAF)[:RMAX])(leaf_keys)
    return picks.astype(jnp.int32)


def draw_ranks(key, part):
    base_key = jax.random.fold_in(key, 23)
    first_key, second_key = jax.random.split(base_key)
    values = jax.random.randint(first_key, (LEAVES,), RMAX // 2, RMAX + 1, dtype=jnp.int32)
    chosen = jax.random.randint(second_key, (), 0, LEAVES, dtype=jnp.int32)
    return values.at[chosen].set(RMAX).astype(jnp.int32)


def draw_owners(key, part):
    base_key = jax.random.fold_in(key, 37)
    first_key, second_key = jax.random.split(base_key)
    shuffled = jax.random.permutation(first_key, PARENTS)
    busiest = jax.random.randint(second_key, (), 0, OWNERS, dtype=jnp.int32)
    position = jnp.arange(PARENTS, dtype=jnp.int32)
    rest = OWNERS - 1
    later = jnp.maximum(position - SLOTS, 0)
    others = jnp.where(later == 0, 0, (rest - 1 + later - 1) % rest).astype(jnp.int32)
    others = others + (others >= busiest).astype(jnp.int32)
    values = jnp.where(position < SLOTS, busiest, others).astype(jnp.int32)
    return jnp.zeros((PARENTS,), jnp.int32).at[shuffled].set(values)


def steps_of(key, shape, pieces, low, largest):
    def one(dim, shards_of):
        draws = jax.random.uniform(jax.random.fold_in(jax.random.fold_in(key, 6), dim), (shards_of,), jnp.float32, low / len(pieces), largest / len(pieces))
        return jnp.repeat(jnp.exp(draws), shape[dim] // shards_of).reshape((-1,) + (1,) * (len(shape) - dim - 1))

    factor_of = one(*pieces[0])
    for cut in pieces[1:]:
        factor_of = factor_of * one(*cut)
    return factor_of


def bell_draw(rng, dims, width, reach, cuts=(), held_as=jnp.bfloat16):
    values = jax.random.normal(rng, dims, jnp.float32) * width
    if len(cuts) > 0:
        values = steps_of(rng, dims, cuts, -0.22, 0.18) * values
    return jnp.clip(values, min=-reach, max=reach).astype(held_as)


def setup_inputs(seed: int = 0) -> dict:
    splits = jax.random.split(jax.random.key(seed), 6)
    return {
        "points": draw_points(jax.random.fold_in(splits[5], 71), 0),
        "omega": bell_draw(splits[1], (N, S), N ** -0.5, 0.0234375, ((0, 32),)),
        "pivots": draw_pivots(jax.random.fold_in(splits[5], 71), 0),
        "ranks": draw_ranks(jax.random.fold_in(splits[5], 71), 0),
        "owners": draw_owners(jax.random.fold_in(splits[5], 71), 0),
    }


soften = 0.0001
highest = lax.Precision.HIGHEST

def kernel_block(row_pts, col_pts):
    dist_sq = (row_pts[0][:, None] - col_pts[0][None, :]) ** 2
    dist_sq = dist_sq + (row_pts[1][:, None] - col_pts[1][None, :]) ** 2
    dist_sq = dist_sq + (row_pts[2][:, None] - col_pts[2][None, :]) ** 2
    return 1.0 / jnp.sqrt(dist_sq + soften)

def reference(points, omega, pivots, ranks, owners):
    count_all = points.shape[1]
    row_blk = math.gcd(count_all, 1024)
    col_leaf = jnp.arange(count_all, dtype=jnp.int32) // LEAF

    def row_block(number):
        first_row = number * row_blk
        row_pts = lax.dynamic_slice_in_dim(points, first_row, row_blk, 1)
        row_leaf = (first_row + jnp.arange(row_blk, dtype=jnp.int32)) // LEAF
        kernel = kernel_block(row_pts, points)
        kernel = jnp.where(row_leaf[:, None] == col_leaf[None, :], 0.0, kernel).astype(jnp.bfloat16)
        return jnp.dot(kernel.astype(jnp.float32), omega.astype(jnp.float32), preferred_element_type=jnp.float32)
    samples = lax.map(row_block, jnp.arange(count_all // row_blk, dtype=jnp.int32)).reshape(LEAVES, LEAF, S)
    live_mask = jnp.arange(RMAX, dtype=jnp.int32)[None, :] < ranks[:, None]
    skeleton = jax.vmap(lambda leaf_rows, picks: leaf_rows[picks])(samples, pivots)
    skeleton = jnp.where(live_mask[:, :, None], skeleton, 0.0)

    def sibling(leaf_id):
        sibling_leaf = jnp.bitwise_xor(leaf_id, 1)
        piv_pts = points[:, leaf_id * LEAF + pivots[leaf_id]]
        col_pts = lax.dynamic_slice_in_dim(points, sibling_leaf * LEAF, LEAF, 1)
        sketch = lax.dynamic_slice_in_dim(omega, sibling_leaf * LEAF, LEAF, 0)
        kernel = kernel_block(piv_pts, col_pts).astype(jnp.bfloat16)
        return jnp.dot(kernel.astype(jnp.float32), sketch.astype(jnp.float32), preferred_element_type=jnp.float32)
    correction = lax.map(sibling, jnp.arange(LEAVES, dtype=jnp.int32))
    correction = jnp.where(live_mask[:, :, None], correction, 0.0)
    reduced = skeleton - correction

    def interpolate(packed):
        leaf_rows, skel_rows, rank_of = packed
        gram_mat = jnp.dot(skel_rows, skel_rows.T, precision=highest)
        ridge_term = 0.1 * jnp.trace(gram_mat) / rank_of.astype(jnp.float32) + 1e-06
        gram_mat = gram_mat + ridge_term * jnp.eye(RMAX, dtype=jnp.float32)
        factor = jnp.linalg.cholesky(gram_mat)
        right_side = jnp.dot(leaf_rows, skel_rows.T, precision=highest)
        return jax.scipy.linalg.cho_solve((factor, True), right_side.T).T
    interp = lax.map(interpolate, (samples, skeleton, ranks)).reshape(LEAVES * LEAF, RMAX)
    paired = reduced.reshape(PARENTS, 2 * RMAX, S)
    parent_ids = jnp.arange(PARENTS, dtype=jnp.int32)
    shared = owners[:, None] == owners[None, :]
    slot_of = lax.optimization_barrier(jnp.sum(shared & (parent_ids[None, :] < parent_ids[:, None]), axis=1)).astype(jnp.int32)
    placed = jnp.zeros((OWNERS, SLOTS, 2 * RMAX, S), jnp.float32).at[owners, slot_of].set(paired)
    return (interp, placed)
```

```python
import functools

import jax
import jax.numpy as jnp
from jax import lax
from jax.experimental import pallas as pl
from jax.experimental.pallas import tpu as pltpu
from jax.sharding import PartitionSpec as P

BF = jnp.bfloat16
F32 = jnp.float32
MESH = pl.DeviceIdType.MESH
HIGHEST = lax.Precision.HIGHEST
SOFTEN = 0.0001
DEPTH = 32
WAYS = 4
LEAF = 2048
SLAB = 512
S = 256
RMAX = 256
PIECE = 64
HALF = 1024


def place():
    y = lax.axis_index("grp")
    d = lax.axis_index("dev")
    return y, d // 8, (d // 2) % 4, d % 2


def dev_of(z, x, c):
    return ((z % 4) * 4 + (x % 4)) * 2 + c


SPLIT_PAIRS = [(0, 0), (0, 1), (1, 0), (1, 1), (0, 2), (2, 0), (1, 2), (2, 1)]


def splits(value):
    high = value.astype(BF).astype(F32)
    rest = value - high
    mid = rest.astype(BF).astype(F32)
    return [high, mid, rest - mid]


def distance_rows(coords, col_side):
    n = coords.shape[1]
    row = lax.broadcasted_iota(jnp.int32, (8, n), 0)
    norm = jnp.sum(coords * coords, axis=0, keepdims=True)
    twice = coords + pltpu.roll(coords, 3, 0)
    if col_side:
        value = jnp.where(row < 6, -2.0 * twice, jnp.where(row == 6, 1.0, norm + SOFTEN))
    else:
        value = jnp.where(row < 6, twice, jnp.where(row == 6, norm, 1.0))
    parts = splits(value)
    side, varying = (1, 7) if col_side else (0, 6)
    blocks = []
    for g in range(4):
        first, second = SPLIT_PAIRS[2 * g][side], SPLIT_PAIRS[2 * g + 1][side]
        block = jnp.where(row < 3, parts[first], parts[second])
        if g < 3:
            block = jnp.where(row >= 6, jnp.where(row == varying, parts[g], 1.0), block)
        else:
            block = jnp.where(row >= 6, 0.0, block)
        blocks.append(block)
    return jnp.concatenate(blocks, axis=0)


def centred(block):
    n = block.shape[1]
    return jnp.concatenate([block - 0.5, jnp.zeros((5, n), F32)], axis=0)


def sweep_kernel(
    pts, om_in, pivots, ranks,
    s_out, skel_out, par_out,
    cp, rp, om, arow, apiv, bcol, acc, accp, kb0, kb1, sbuf, rbuf, prbuf, skel, red, par,
    own_sem, cps, cpr, rps, rpr, oms, omr, fws, rds, rdr, pvs, pvr, sks, skr, pas, par_sem,
):
    y, z, x, c = place()
    dirs = [(1, 0), (0, 1), (0, 3)]

    def block_chip(j):
        return (x + j) % 4, (z + 2 * (j % 2)) % 4

    def block_leaf(j):
        xr, zr = block_chip(j)
        return y * 8 + 2 * zr + xr // 2

    def to(dev, grp=None):
        return (y if grp is None else grp, dev)

    me = dev_of(z, x, c)
    own_copy = pltpu.make_async_copy(om_in, om.at[0], own_sem)
    own_copy.start()
    barrier = pltpu.get_barrier_semaphore()
    for k in range(1, 32):
        pl.semaphore_signal(barrier, inc=1, device_id=to((me + k) % 32), device_id_type=MESH)
    for gy in range(1, 4):
        for zs in range(4):
            pl.semaphore_signal(
                barrier, inc=1, device_id=to(dev_of(zs, z, x // 2), (y + gy) % 4), device_id_type=MESH
            )
    cp[0] = pts[...]
    pl.semaphore_wait(barrier, 43)

    def row_copy(i, j, core):
        xr, zr = 2 * c + i, x
        return pltpu.make_async_remote_copy(
            src_ref=pts, dst_ref=rp.at[j], send_sem=rps.at[i * 8 + j * 2 + core], recv_sem=rpr.at[j],
            device_id=to(dev_of(zr - 2 * (j % 2) + 4, xr - j + 4, core)), device_id_type=MESH,
        )

    def row_target(i, j, core):
        return dev_of(x - 2 * (j % 2) + 4, 2 * c + i - j + 4, core)

    @pl.when(z == y)
    def _():
        for i in range(2):
            for j in range(WAYS):
                for core in range(2):
                    self_target = row_target(i, j, core) == me

                    @pl.when(self_target)
                    def _():
                        pltpu.make_async_copy(pts, rp.at[j], rpr.at[j]).start()

                    @pl.when(jnp.logical_not(self_target))
                    def _():
                        row_copy(i, j, core).start()

    def col_copies():
        copies = [
            pltpu.make_async_remote_copy(
                src_ref=pts, dst_ref=cp.at[1], send_sem=cps.at[0], recv_sem=cpr.at[1],
                device_id=to(dev_of(z, x, 1 - c)), device_id_type=MESH,
            )
        ]
        for i, (dx, dz) in enumerate(dirs):
            for other in range(2):
                core = c if other == 0 else 1 - c
                copies.append(
                    pltpu.make_async_remote_copy(
                        src_ref=pts, dst_ref=cp.at[2 + 2 * i + other],
                        send_sem=cps.at[1 + 2 * i + other], recv_sem=cpr.at[2 + 2 * i + other],
                        device_id=to(dev_of(z - dz + 4, x - dx + 4, core)), device_id_type=MESH,
                    )
                )
        return copies

    col_sends = col_copies()
    for copy in col_sends:
        copy.start()

    def om_send(i, half):
        rows = pl.ds(half * HALF, HALF)
        if i == 0:
            slot, dev = 1, dev_of(z, x, 1 - c)
        else:
            dx, dz = dirs[i - 1]
            slot, dev = 2 * i, dev_of(z - dz + 4, x - dx + 4, c)
        return pltpu.make_async_remote_copy(
            src_ref=om_in.at[rows], dst_ref=om.at[slot, rows], send_sem=oms.at[i, half],
            recv_sem=omr.at[slot, half], device_id=to(dev), device_id_type=MESH,
        )

    for half in range(2):
        for i in range(4):
            om_send(i, half).start()

    def forward(slot, half):
        rows = pl.ds(half * HALF, HALF)
        return pltpu.make_async_remote_copy(
            src_ref=om.at[slot, rows], dst_ref=om.at[slot + 1, rows], send_sem=fws.at[slot // 2 - 1, half],
            recv_sem=omr.at[slot + 1, half], device_id=to(dev_of(z, x, 1 - c)), device_id_type=MESH,
        )

    def om_arrived(slot, half):
        rows = pl.ds(half * HALF, HALF)
        pltpu.make_async_copy(om.at[slot, rows], om.at[slot, rows], omr.at[slot, half]).wait()

    def build_col(slot):
        bcol[slot] = distance_rows(centred(cp[slot]), True).astype(BF)

    build_col(0)

    pick_acc = [jnp.zeros((8, 128), F32), jnp.zeros((8, 128), F32)]
    for j in range(WAYS):
        pltpu.make_async_copy(rp.at[j], rp.at[j], rpr.at[j]).wait()
        xr, zr = block_chip(j)
        start = pl.multiple_of(((xr % 2) * 2 + c) * SLAB, SLAB)
        arow[j] = distance_rows(centred(rp[j, :, pl.ds(start, SLAB)]), False).T.astype(BF)
        whole = centred(rp[j])
        split = jnp.concatenate([*splits(whole), jnp.zeros((8, LEAF), F32)], axis=0).astype(BF)
        piv = jnp.broadcast_to(pivots[pl.ds(block_leaf(j), 1), :], (8, RMAX))
        piv = jnp.where(xr % 2 == 0, piv[:, :128], piv[:, 128:])
        piv = jnp.where(c == j % 2, piv, pltpu.roll(piv, 64, 1))
        lane = lax.broadcasted_iota(jnp.int32, (8, 128), 1)
        piv = jnp.where(lane // 64 == j % 2, piv, -1)
        here = lax.broadcasted_iota(jnp.int32, (LEAF, 128), 0) == piv[:1]
        hit = jnp.dot(split, here.astype(BF), preferred_element_type=F32)
        pick_acc[j // 2] = pick_acc[j // 2] + (hit[0:8] + hit[8:16] + hit[16:24])
    for t in range(2):
        apiv[t * 128 : (t + 1) * 128] = distance_rows(pick_acc[t], False).T.astype(BF)
    for slot in range(1, 8):
        pltpu.make_async_copy(cp.at[slot], cp.at[slot], cpr.at[slot]).wait()
        build_col(slot)
    own_copy.wait()

    acc[...] = jnp.zeros_like(acc)
    accp[...] = jnp.zeros_like(accp)

    def nth(i):
        k = (i - 4) % 6
        late = i >= 4
        slot = jnp.where(late, jnp.where(k < 3, 2 + 2 * k, 3 + 2 * (k - 3)), i // 2)
        half = jnp.where(late, (i - 4) // 6, i % 2)
        return slot, half

    def slot_leaf(slot):
        pair = slot // 2
        xq = jnp.where(pair == 1, x + 1, x) % 4
        zq = (z + jnp.where(pair == 2, 1, jnp.where(pair == 3, 3, 0))) % 4
        cq = jnp.where(slot % 2 == 0, c, 1 - c)
        return dev_of(zq, xq, cq)

    def gen(rows, slot, half, kb):
        cols = pl.ds(pl.multiple_of(half * HALF, HALF), HALF)
        dist = jnp.dot(rows, bcol[slot, :, cols], preferred_element_type=F32)
        kb[...] = lax.rsqrt(dist).astype(BF)

    def product(slot, half, kb):
        rows = pl.ds(pl.multiple_of(half * HALF, HALF), HALF)
        return jnp.dot(kb[...], om[slot, rows, :], preferred_element_type=F32)

    def use_main(slot, half, j, kb):
        keep = jnp.where(slot_leaf(slot) == block_leaf(j), 0.0, 1.0).astype(F32)
        acc[j] += keep * product(slot, half, kb)

    def ready(i):
        slot, half = nth(i)

        @pl.when(i >= 2)
        def _():
            om_arrived(slot, half)

        @pl.when(jnp.logical_and(slot >= 2, slot % 2 == 0))
        def _():
            forward(slot, half).start()

    gen(arow[0], 0, 0, kb0)

    @pl.loop(0, 20)
    def _(t):
        i = t // 2
        j = (t % 2) * 2
        slot, half = nth(i)

        @pl.when(t % 2 == 0)
        def _():
            ready(i)

        gen(arow[j + 1], slot, half, kb1)
        use_main(slot, half, j, kb0)
        nxt = jnp.minimum(t + 1, 19)
        nslot, nhalf = nth(nxt // 2)
        gen(arow[(nxt % 2) * 2], nslot, nhalf, kb0)
        use_main(slot, half, j + 1, kb1)

    for i in range(10, 13):
        ready(jnp.int32(i))
    kp0, kp1 = kb0.at[pl.ds(0, RMAX)], kb1.at[pl.ds(0, RMAX)]

    def use_piv(slot, half, kb):
        got = product(slot, half, kb)
        for j in range(WAYS):
            own = slot_leaf(slot) == block_leaf(j)
            sib = dev_of(slot_leaf(slot) // 8, (slot_leaf(slot) // 2) % 4, 1 - slot_leaf(slot) % 2) == block_leaf(j)
            part = got[j * PIECE : (j + 1) * PIECE]
            accp[j, 0] += jnp.where(jnp.logical_or(own, sib), 0.0, 1.0).astype(F32) * part
            accp[j, 1] += jnp.where(sib, 1.0, 0.0).astype(F32) * part

    gen(apiv[...], 0, 0, kp0)

    @pl.loop(0, 8)
    def _(t):
        @pl.when(t >= 6)
        def _():
            for e in range(2):
                @pl.when(2 * t + e >= 13)
                def _():
                    slot, half = nth(2 * t + e)
                    om_arrived(slot, half)

        slot, half = nth(2 * t)
        slot1, half1 = nth(2 * t + 1)
        gen(apiv[...], slot1, half1, kp1)
        use_piv(slot, half, kp0)
        slot2, half2 = nth(jnp.minimum(2 * t + 2, 15))
        gen(apiv[...], slot2, half2, kp0)
        use_piv(slot1, half1, kp1)

    def piv_send(j):
        xr, zr = block_chip(j)
        return pltpu.make_async_remote_copy(
            src_ref=accp.at[j], dst_ref=prbuf.at[j - 1], send_sem=pvs.at[j - 1], recv_sem=pvr.at[j - 1],
            device_id=to(dev_of(zr, xr, c)), device_id_type=MESH,
        )

    for j in range(1, WAYS):
        piv_send(j).start()

    def main_send(j):
        xr, zr = block_chip(j)
        return pltpu.make_async_remote_copy(
            src_ref=sbuf.at[j - 1], dst_ref=rbuf.at[j - 1], send_sem=rds.at[j - 1], recv_sem=rdr.at[j - 1],
            device_id=to(dev_of(zr, xr, c)), device_id_type=MESH,
        )

    piece = 2 * (x % 2) + c
    piece_rows = pl.ds(pl.multiple_of(piece * PIECE, PIECE), PIECE)

    def skel_send(k):
        xs = x if k == 0 else x + 1 - 2 * (x % 2)
        core = 1 - c if k != 1 else c
        return pltpu.make_async_remote_copy(
            src_ref=skel.at[piece_rows], dst_ref=skel.at[piece_rows], send_sem=sks.at[k], recv_sem=skr.at[k],
            device_id=to(dev_of(z, xs, core)), device_id_type=MESH,
        )

    def par_dev(k):
        return dev_of(x, 2 * c + k // 2, k % 2)

    def par_send(k, g):
        return pltpu.make_async_remote_copy(
            src_ref=red.at[pl.ds(k * 16, 16)], dst_ref=par.at[4 * y + z], send_sem=pas.at[4 * g + k],
            recv_sem=par_sem.at[4 * y + z], device_id=to(par_dev(k), (y + g) % 4), device_id_type=MESH,
        )

    def finish_pivots():
        for j in range(3):
            pltpu.make_async_copy(prbuf.at[j], prbuf.at[j], pvr.at[j]).wait()
        total = accp[0] + prbuf[0] + prbuf[1] + prbuf[2]
        ids = lax.broadcasted_iota(jnp.int32, (PIECE, S), 0) + piece * PIECE
        live = ids < ranks[block_leaf(0)]
        skel[piece_rows, :] = jnp.where(live, total[0] + total[1], 0.0)
        red[...] = jnp.where(live, total[0], 0.0)
        for k in range(3):
            skel_send(k).start()
        for k in range(4):
            for g in range(4):
                if g:
                    par_send(k, g).start()
                else:
                    self_target = par_dev(k) == me

                    @pl.when(self_target)
                    def _():
                        pltpu.make_async_copy(
                            red.at[pl.ds(k * 16, 16)], par.at[4 * y + z], par_sem.at[4 * y + z]
                        ).start()

                    @pl.when(jnp.logical_not(self_target))
                    def _():
                        par_send(k, g).start()

    gen(arow[1], 2, 1, kb0)

    @pl.loop(0, 12)
    def _(t):
        j = (t // 3 + 1) % 4
        i = 10 + 2 * (t % 3)

        @pl.when(t == 4)
        def _():
            finish_pivots()

        slot, half = nth(i)
        slot1, half1 = nth(i + 1)
        gen(arow[j], slot1, half1, kb1)
        use_main(slot, half, j, kb0)
        nxt = jnp.minimum(t + 1, 11)
        slot2, half2 = nth(10 + 2 * (nxt % 3))
        gen(arow[(nxt // 3 + 1) % 4], slot2, half2, kb0)
        use_main(slot1, half1, j, kb1)
        for jj in range(1, WAYS):
            @pl.when(t == 3 * jj - 1)
            def _():
                sbuf[jj - 1] = acc[jj].astype(BF)
                main_send(jj).start()

    for j in range(3):
        pltpu.make_async_copy(rbuf.at[j], rbuf.at[j], rdr.at[j]).wait()
    s_out[...] = acc[0] + (rbuf[0].astype(F32) + rbuf[1].astype(F32)) + rbuf[2].astype(F32)
    for k in range(3):
        pltpu.make_async_copy(skel.at[pl.ds(0, PIECE)], skel.at[pl.ds(0, PIECE)], skr.at[k]).wait()
    skel_out[...] = skel[...]
    for q in range(16):
        pltpu.make_async_copy(par.at[q], par.at[q], par_sem.at[q]).wait()
    par_out[...] = par[...]

    @pl.when(z == y)
    def _():
        for i in range(2):
            for j in range(WAYS):
                for core in range(2):
                    @pl.when(row_target(i, j, core) != me)
                    def _():
                        row_copy(i, j, core).wait_send()

    for copy in col_sends:
        copy.wait_send()
    for half in range(2):
        for i in range(4):
            om_send(i, half).wait_send()
        for i in range(3):
            forward(2 + 2 * i, half).wait_send()
    for j in range(1, WAYS):
        piv_send(j).wait_send()
        main_send(j).wait_send()
    for k in range(3):
        skel_send(k).wait_send()
    for k in range(4):
        for g in range(4):
            if g:
                par_send(k, g).wait_send()
            else:
                @pl.when(par_dev(k) != me)
                def _():
                    par_send(k, g).wait_send()


def hdot(a, b, dims):
    return lax.dot_general(a, b, (dims, ((), ())), precision=HIGHEST, preferred_element_type=F32)


def solve_kernel(samples, skel, par, ranks, owners, interp, placed):
    y, z, x, c = place()
    rows = skel[...]
    gram = hdot(rows, rows, ((1,), (1,)))
    squares = jnp.sum(rows * rows, axis=1, keepdims=True)
    trace = jnp.sum(squares, axis=0, keepdims=True)
    rank = ranks[y * 8 + 2 * z + x // 2].astype(F32)
    low = 0.1 * trace / rank + 1e-06
    eye = lax.broadcasted_iota(jnp.int32, (RMAX, RMAX), 0) == lax.broadcasted_iota(jnp.int32, (RMAX, RMAX), 1)
    gram = gram + jnp.where(eye, low, 0.0)
    high = low + trace
    a = 2.0 / (low + high)
    ratio = low / high
    inv = None
    for step in range(9):
        gap = (1.0 - ratio) / (1.0 + ratio)
        grow = 2.0 / (2.0 - gap * gap)
        if inv is None:
            inv = grow * (jnp.where(eye, 2.0 * a, 0.0) - a * a * gram)
        else:
            prod = hdot(gram, inv, ((1,), (0,)))
            inv = grow * hdot(inv, jnp.where(eye, 2.0, 0.0) - prod, ((1,), (0,)))
        ratio = 1.0 - gap * gap
    basis = hdot(inv, rows, ((1,), (0,)))
    interp[...] = hdot(samples[...], basis, ((1,), (1,)))
    placed[...] = jnp.zeros_like(placed)
    count = jnp.int32(0)
    for q in range(16):
        mine = owners[q] == y

        @pl.when(mine)
        def _():
            placed[0, count] = par[q]

        count = count + jnp.where(mine, 1, 0)


def body(points, omega, pivots, ranks, owners):
    vmem = pl.BlockSpec(memory_space=pltpu.VMEM)
    smem = pl.BlockSpec(memory_space=pltpu.SMEM)
    dma = pltpu.SemaphoreType.DMA
    samples, skel, par = pl.pallas_call(
        sweep_kernel,
        name="sweep",
        out_shape=[
            jax.ShapeDtypeStruct((SLAB, S), F32),
            jax.ShapeDtypeStruct((RMAX, S), F32),
            jax.ShapeDtypeStruct((16, 16, S), F32),
        ],
        in_specs=[vmem, pl.BlockSpec(memory_space=pl.ANY), vmem, smem],
        out_specs=[vmem, vmem, vmem],
        scratch_shapes=[
            pltpu.VMEM((8, 3, LEAF), F32),
            pltpu.VMEM((4, 3, LEAF), F32),
            pltpu.VMEM((8, LEAF, S), BF),
            pltpu.VMEM((4, SLAB, DEPTH), BF),
            pltpu.VMEM((RMAX, DEPTH), BF),
            pltpu.VMEM((8, DEPTH, LEAF), BF),
            pltpu.VMEM((4, SLAB, S), F32),
            pltpu.VMEM((4, 2, PIECE, S), F32),
            pltpu.VMEM((SLAB, HALF), BF),
            pltpu.VMEM((SLAB, HALF), BF),
            pltpu.VMEM((3, SLAB, S), BF),
            pltpu.VMEM((3, SLAB, S), BF),
            pltpu.VMEM((3, 2, PIECE, S), F32),
            pltpu.VMEM((RMAX, S), F32),
            pltpu.VMEM((PIECE, S), F32),
            pltpu.VMEM((16, 16, S), F32),
            dma, dma((7,)), dma((8,)), dma((16,)), dma((4,)), dma((4, 2)), dma((8, 2)), dma((3, 2)),
            dma((3,)), dma((3,)), dma((3,)), dma((3,)), dma((3,)), dma((3,)), dma((16,)), dma((16,)),
        ],
        compiler_params=pltpu.CompilerParams(
            collective_id=0, has_side_effects=True, vmem_limit_bytes=56 * 2**20
        ),
    )(points, omega, pivots, ranks)
    interp, placed = pl.pallas_call(
        solve_kernel,
        name="solve",
        out_shape=[
            jax.ShapeDtypeStruct((SLAB, RMAX), F32),
            jax.ShapeDtypeStruct((1, 8, 16, S), F32),
        ],
        in_specs=[vmem, vmem, vmem, smem, smem],
        out_specs=[vmem, vmem],
        compiler_params=pltpu.CompilerParams(vmem_limit_bytes=32 * 2**20),
    )(samples, skel, par, ranks, owners)
    return interp, placed


def solution(mesh):
    placed = (P(None, "dev"), P("dev", None), P(), P(), P())
    return jax.shard_map(
        body,
        mesh=mesh,
        in_specs=placed,
        out_specs=(P(("grp", "dev"), None), P("grp", None, "dev", None)),
        check_vma=False,
    )
```

```python
import functools

import jax
import jax.numpy as jnp
from jax import lax
from jax.experimental import pallas as pl
from jax.experimental.pallas import tpu as pltpu
from jax.sharding import PartitionSpec as P

BF = jnp.bfloat16
F32 = jnp.float32
MESH = pl.DeviceIdType.MESH
HIGHEST = lax.Precision.HIGHEST
SOFTEN = 0.0001
DEPTH = 32
WAYS = 4
LEAF = 2048
SLAB = 512
S = 256
RMAX = 256
PIECE = 64
HALF = 1024


def place():
    y = lax.axis_index("grp")
    d = lax.axis_index("dev")
    return y, d // 8, (d // 2) % 4, d % 2


def dev_of(z, x, c):
    return ((z % 4) * 4 + (x % 4)) * 2 + c


SPLIT_PAIRS = [(0, 0), (0, 1), (1, 0), (1, 1), (0, 2), (2, 0), (1, 2), (2, 1)]


def splits(value):
    high = value.astype(BF).astype(F32)
    rest = value - high
    mid = rest.astype(BF).astype(F32)
    return [high, mid, rest - mid]


def distance_rows(coords, col_side):
    n = coords.shape[1]
    row = lax.broadcasted_iota(jnp.int32, (8, n), 0)
    norm = jnp.sum(coords * coords, axis=0, keepdims=True)
    twice = coords + pltpu.roll(coords, 3, 0)
    if col_side:
        value = jnp.where(row < 6, -2.0 * twice, jnp.where(row == 6, 1.0, norm + SOFTEN))
    else:
        value = jnp.where(row < 6, twice, jnp.where(row == 6, norm, 1.0))
    parts = splits(value)
    side, varying = (1, 7) if col_side else (0, 6)
    blocks = []
    for g in range(4):
        first, second = SPLIT_PAIRS[2 * g][side], SPLIT_PAIRS[2 * g + 1][side]
        block = jnp.where(row < 3, parts[first], parts[second])
        if g < 3:
            block = jnp.where(row >= 6, jnp.where(row == varying, parts[g], 1.0), block)
        else:
            block = jnp.where(row >= 6, 0.0, block)
        blocks.append(block)
    return jnp.concatenate(blocks, axis=0)


def centred(block):
    n = block.shape[1]
    return jnp.concatenate([block - 0.5, jnp.zeros((5, n), F32)], axis=0)


def hdot(a, b, dims):
    return lax.dot_general(a, b, (dims, ((), ())), precision=HIGHEST, preferred_element_type=F32)


def dot3(a, b, dims):
    def one(p, q):
        return lax.dot_general(p, q, (dims, ((), ())), preferred_element_type=F32)

    ah, bh = a.astype(BF), b.astype(BF)
    al, bl = (a - ah.astype(F32)).astype(BF), (b - bh.astype(F32)).astype(BF)
    return one(ah, bh) + (one(ah, bl) + one(al, bh))


def interp_basis(rows, rank):
    gram = hdot(rows, rows, ((1,), (1,)))
    squares = jnp.sum(rows * rows, axis=1, keepdims=True)
    trace = jnp.sum(squares, axis=0, keepdims=True)
    low = 0.1 * trace / rank + 1e-06
    eye = lax.broadcasted_iota(jnp.int32, (RMAX, RMAX), 0) == lax.broadcasted_iota(jnp.int32, (RMAX, RMAX), 1)
    gram = gram + jnp.where(eye, low, 0.0)
    high = low + trace
    a = 2.0 / (low + high)
    ratio = low / high
    inv = None
    for step in range(9):
        gap = (1.0 - ratio) / (1.0 + ratio)
        grow = 2.0 / (2.0 - gap * gap)
        if inv is None:
            inv = grow * (jnp.where(eye, 2.0 * a, 0.0) - a * a * gram)
        else:
            mul = dot3 if step < 6 else hdot
            prod = mul(gram, inv, ((1,), (0,)))
            inv = grow * mul(inv, jnp.where(eye, 2.0, 0.0) - prod, ((1,), (0,)))
        ratio = 1.0 - gap * gap
    return hdot(inv, rows, ((1,), (0,)))


def sweep_kernel(
    pts, om_in, pivots, ranks, owners,
    interp, placed,
    packed, outbox, inbox, cp, om, arow, apiv, bcol, acc, accp, kb0, kb1, sbuf, rbuf, prbuf, skel, red, par,
    own_sem, cps, cpr, rps, rpr, oms, omr, fws, rds, rdr, pvs, pvr, sks, skr, pas, par_sem,
):
    y, z, x, c = place()
    dirs = [(1, 0), (0, 1), (0, 3)]

    def block_chip(j):
        return (x + j) % 4, (z + 2 * (j % 2)) % 4

    def block_leaf(j):
        xr, zr = block_chip(j)
        return y * 8 + 2 * zr + xr // 2

    def to(dev, grp=None):
        return (y if grp is None else grp, dev)

    me = dev_of(z, x, c)
    own_copy = pltpu.make_async_copy(om_in, om.at[0], own_sem)
    own_copy.start()
    barrier = pltpu.get_barrier_semaphore()
    for k in range(1, 32):
        pl.semaphore_signal(barrier, inc=1, device_id=to((me + k) % 32), device_id_type=MESH)
    for gy in range(1, 4):
        for zs in range(4):
            pl.semaphore_signal(
                barrier, inc=1, device_id=to(dev_of(zs, z, x // 2), (y + gy) % 4), device_id_type=MESH
            )

    whole = centred(pts[...])
    packed[...] = whole[:, :HALF] + pltpu.roll(whole[:, HALF:], 3, 0)
    split = jnp.concatenate([*splits(whole), jnp.zeros((8, LEAF), F32)], axis=0).astype(BF)
    wanted = pivots[pl.ds(me, 1), :]
    here = lax.broadcasted_iota(jnp.int32, (LEAF, RMAX), 0) == wanted
    hit = jnp.dot(split, here.astype(BF), preferred_element_type=F32)
    picked = hit[0:8] + hit[8:16] + hit[16:24]
    first64 = lax.broadcasted_iota(jnp.int32, (8, 128), 1) < 64
    for i in range(2):
        tile = picked[:, i * 128 : (i + 1) * 128]
        other = pltpu.roll(tile, 64, 1)
        for core in range(2):
            lo = (2 * i + core) * SLAB
            outbox[i, core, :, : SLAB // 2] = whole[:, lo : lo + SLAB // 2] + pltpu.roll(
                whole[:, lo + SLAB // 2 : lo + SLAB], 3, 0
            )
            outbox[i, core, :, SLAB // 2 :] = jnp.where(first64, tile, other) if core == 0 else jnp.where(first64, other, tile)
    bcol[0] = distance_rows(whole, True).astype(BF)
    pl.semaphore_wait(barrier, 43)

    def row_copy(i, j, core):
        xr, zr = 2 * c + i, x
        return pltpu.make_async_remote_copy(
            src_ref=outbox.at[i, core], dst_ref=inbox.at[j], send_sem=rps.at[i * 8 + j * 2 + core], recv_sem=rpr.at[j],
            device_id=to(dev_of(zr - 2 * (j % 2) + 4, xr - j + 4, core)), device_id_type=MESH,
        )

    def row_target(i, j, core):
        return dev_of(x - 2 * (j % 2) + 4, 2 * c + i - j + 4, core)

    @pl.when(z == y)
    def _():
        for i in range(2):
            for j in range(WAYS):
                for core in range(2):
                    self_target = row_target(i, j, core) == me

                    @pl.when(self_target)
                    def _():
                        pltpu.make_async_copy(outbox.at[i, core], inbox.at[j], rpr.at[j]).start()

                    @pl.when(jnp.logical_not(self_target))
                    def _():
                        row_copy(i, j, core).start()

    def col_copies():
        copies = [
            pltpu.make_async_remote_copy(
                src_ref=packed, dst_ref=cp.at[1], send_sem=cps.at[0], recv_sem=cpr.at[1],
                device_id=to(dev_of(z, x, 1 - c)), device_id_type=MESH,
            )
        ]
        for i, (dx, dz) in enumerate(dirs):
            for other in range(2):
                core = c if other == 0 else 1 - c
                copies.append(
                    pltpu.make_async_remote_copy(
                        src_ref=packed, dst_ref=cp.at[2 + 2 * i + other],
                        send_sem=cps.at[1 + 2 * i + other], recv_sem=cpr.at[2 + 2 * i + other],
                        device_id=to(dev_of(z - dz + 4, x - dx + 4, core)), device_id_type=MESH,
                    )
                )
        return copies

    col_sends = col_copies()
    for copy in col_sends:
        copy.start()

    def om_send(i, half):
        rows = pl.ds(half * HALF, HALF)
        if i == 0:
            slot, dev = 1, dev_of(z, x, 1 - c)
        else:
            dx, dz = dirs[i - 1]
            slot, dev = 2 * i, dev_of(z - dz + 4, x - dx + 4, c)
        return pltpu.make_async_remote_copy(
            src_ref=om_in.at[rows], dst_ref=om.at[slot, rows], send_sem=oms.at[i, half],
            recv_sem=omr.at[slot, half], device_id=to(dev), device_id_type=MESH,
        )

    for half in range(2):
        for i in range(4):
            om_send(i, half).start()

    def forward(slot, half):
        rows = pl.ds(half * HALF, HALF)
        return pltpu.make_async_remote_copy(
            src_ref=om.at[slot, rows], dst_ref=om.at[slot + 1, rows], send_sem=fws.at[slot // 2 - 1, half],
            recv_sem=omr.at[slot + 1, half], device_id=to(dev_of(z, x, 1 - c)), device_id_type=MESH,
        )

    def om_arrived(slot, half):
        rows = pl.ds(half * HALF, HALF)
        pltpu.make_async_copy(om.at[slot, rows], om.at[slot, rows], omr.at[slot, half]).wait()

    xyz = lax.broadcasted_iota(jnp.int32, (8, 1), 0) < 3

    def build_col(slot):
        pltpu.make_async_copy(cp.at[slot], cp.at[slot], cpr.at[slot]).wait()
        both = cp[slot]
        for h in range(2):
            coords = jnp.where(xyz, both if h == 0 else pltpu.roll(both, 5, 0), 0.0)
            bcol[slot, :, h * HALF : (h + 1) * HALF] = distance_rows(coords, True).astype(BF)

    pick = [None, None]
    for j in range(WAYS):
        pltpu.make_async_copy(inbox.at[j], inbox.at[j], rpr.at[j]).wait()
        got = inbox[j]
        pair = got[:, : SLAB // 2]
        coords = jnp.concatenate([jnp.where(xyz, pair, 0.0), jnp.where(xyz, pltpu.roll(pair, 5, 0), 0.0)], axis=1)
        arow[j] = distance_rows(coords, False).T.astype(BF)
        points = got[:, SLAB // 2 :]
        pick[j // 2] = points if j % 2 == 0 else jnp.where(first64, pick[j // 2], points)
    for t in range(2):
        apiv[t * 128 : (t + 1) * 128] = distance_rows(pick[t], False).T.astype(BF)
    build_col(1)
    own_copy.wait()

    acc[...] = jnp.zeros_like(acc)
    accp[...] = jnp.zeros_like(accp)

    def nth(i):
        k = (i - 4) % 6
        late = i >= 4
        slot = jnp.where(late, jnp.where(k < 3, 2 + 2 * k, 3 + 2 * (k - 3)), i // 2)
        half = jnp.where(late, (i - 4) // 6, i % 2)
        return slot, half

    def slot_leaf(slot):
        pair = slot // 2
        xq = jnp.where(pair == 1, x + 1, x) % 4
        zq = (z + jnp.where(pair == 2, 1, jnp.where(pair == 3, 3, 0))) % 4
        cq = jnp.where(slot % 2 == 0, c, 1 - c)
        return dev_of(zq, xq, cq)

    def gen(rows, slot, half, kb):
        cols = pl.ds(pl.multiple_of(half * HALF, HALF), HALF)
        dist = jnp.dot(rows, bcol[slot, :, cols], preferred_element_type=F32)
        kb[...] = lax.rsqrt(dist).astype(BF)

    def product(slot, half, kb):
        rows = pl.ds(pl.multiple_of(half * HALF, HALF), HALF)
        return jnp.dot(kb[...], om[slot, rows, :], preferred_element_type=F32)

    def use_main(slot, half, j, kb):
        keep = jnp.where(slot_leaf(slot) == block_leaf(j), 0.0, 1.0).astype(F32)
        acc[j] += keep * product(slot, half, kb)

    def ready(i):
        slot, half = nth(i)

        @pl.when(i >= 2)
        def _():
            om_arrived(slot, half)

        @pl.when(jnp.logical_and(slot >= 2, slot % 2 == 0))
        def _():
            forward(slot, half).start()

    gen(arow[0], 0, 0, kb0)

    @pl.loop(0, 20)
    def _(t):
        i = t // 2
        j = (t % 2) * 2
        slot, half = nth(i)

        @pl.when(t % 2 == 0)
        def _():
            ready(i)

            @pl.when(jnp.logical_and(i >= 3, i < 9))
            def _():
                build_col(nth(i + 1)[0])

        @pl.when(t == 16)
        def _():
            for late in range(10, 13):
                ready(jnp.int32(late))

        gen(arow[j + 1], slot, half, kb1)
        use_main(slot, half, j, kb0)
        nxt = jnp.minimum(t + 1, 19)
        nslot, nhalf = nth(nxt // 2)
        gen(arow[(nxt % 2) * 2], nslot, nhalf, kb0)
        use_main(slot, half, j + 1, kb1)

    kp0, kp1 = kb0.at[pl.ds(0, RMAX)], kb1.at[pl.ds(0, RMAX)]

    def use_piv(slot, half, kb):
        got = product(slot, half, kb)
        for j in range(WAYS):
            own = slot_leaf(slot) == block_leaf(j)
            sib = dev_of(slot_leaf(slot) // 8, (slot_leaf(slot) // 2) % 4, 1 - slot_leaf(slot) % 2) == block_leaf(j)
            part = got[j * PIECE : (j + 1) * PIECE]
            accp[j, 0] += jnp.where(jnp.logical_or(own, sib), 0.0, 1.0).astype(F32) * part
            accp[j, 1] += jnp.where(sib, 1.0, 0.0).astype(F32) * part

    gen(apiv[...], 0, 0, kp0)

    @pl.loop(0, 8)
    def _(t):
        @pl.when(t >= 6)
        def _():
            for e in range(2):
                @pl.when(2 * t + e >= 13)
                def _():
                    slot, half = nth(2 * t + e)
                    om_arrived(slot, half)

        slot, half = nth(2 * t)
        slot1, half1 = nth(2 * t + 1)
        gen(apiv[...], slot1, half1, kp1)
        use_piv(slot, half, kp0)
        slot2, half2 = nth(jnp.minimum(2 * t + 2, 15))
        gen(apiv[...], slot2, half2, kp0)
        use_piv(slot1, half1, kp1)

    def piv_send(j):
        xr, zr = block_chip(j)
        return pltpu.make_async_remote_copy(
            src_ref=accp.at[j], dst_ref=prbuf.at[j - 1], send_sem=pvs.at[j - 1], recv_sem=pvr.at[j - 1],
            device_id=to(dev_of(zr, xr, c)), device_id_type=MESH,
        )

    for j in range(1, WAYS):
        piv_send(j).start()

    def main_send(j):
        xr, zr = block_chip(j)
        return pltpu.make_async_remote_copy(
            src_ref=sbuf.at[j - 1], dst_ref=rbuf.at[j - 1], send_sem=rds.at[j - 1], recv_sem=rdr.at[j - 1],
            device_id=to(dev_of(zr, xr, c)), device_id_type=MESH,
        )

    piece = 2 * (x % 2) + c
    piece_rows = pl.ds(pl.multiple_of(piece * PIECE, PIECE), PIECE)

    def skel_send(k):
        xs = x if k == 0 else x + 1 - 2 * (x % 2)
        core = 1 - c if k != 1 else c
        return pltpu.make_async_remote_copy(
            src_ref=skel.at[piece_rows], dst_ref=skel.at[piece_rows], send_sem=sks.at[k], recv_sem=skr.at[k],
            device_id=to(dev_of(z, xs, core)), device_id_type=MESH,
        )

    def par_dev(k):
        return dev_of(x, 2 * c + k // 2, k % 2)

    def par_send(k, g):
        return pltpu.make_async_remote_copy(
            src_ref=red.at[pl.ds(k * 16, 16)], dst_ref=par.at[4 * y + z], send_sem=pas.at[4 * g + k],
            recv_sem=par_sem.at[4 * y + z], device_id=to(par_dev(k), (y + g) % 4), device_id_type=MESH,
        )

    def finish_pivots():
        for j in range(3):
            pltpu.make_async_copy(prbuf.at[j], prbuf.at[j], pvr.at[j]).wait()
        total = accp[0] + prbuf[0] + prbuf[1] + prbuf[2]
        ids = lax.broadcasted_iota(jnp.int32, (PIECE, S), 0) + piece * PIECE
        live = ids < ranks[block_leaf(0)]
        skel[piece_rows, :] = jnp.where(live, total[0] + total[1], 0.0)
        red[...] = jnp.where(live, total[0], 0.0)
        for k in range(3):
            skel_send(k).start()
        for k in range(4):
            for g in range(4):
                if g:
                    par_send(k, g).start()
                else:
                    self_target = par_dev(k) == me

                    @pl.when(self_target)
                    def _():
                        pltpu.make_async_copy(
                            red.at[pl.ds(k * 16, 16)], par.at[4 * y + z], par_sem.at[4 * y + z]
                        ).start()

                    @pl.when(jnp.logical_not(self_target))
                    def _():
                        par_send(k, g).start()

    def turn(t):
        k = t // 3
        return jnp.where(k < 2, 1 + 2 * k, 2 * (3 - k))

    gen(arow[1], 2, 1, kb0)

    @pl.loop(0, 12)
    def _(t):
        j = turn(t)
        i = 10 + 2 * (t % 3)

        @pl.when(t == 4)
        def _():
            finish_pivots()

        slot, half = nth(i)
        slot1, half1 = nth(i + 1)
        gen(arow[j], slot1, half1, kb1)
        use_main(slot, half, j, kb0)
        nxt = jnp.minimum(t + 1, 11)
        slot2, half2 = nth(10 + 2 * (nxt % 3))
        gen(arow[turn(nxt)], slot2, half2, kb0)
        use_main(slot1, half1, j, kb1)
        for jj, last in ((1, 2), (3, 5), (2, 8)):
            @pl.when(t == last)
            def _():
                sbuf[jj - 1] = acc[jj].astype(BF)
                main_send(jj).start()

    for k in range(3):
        pltpu.make_async_copy(skel.at[pl.ds(0, PIECE)], skel.at[pl.ds(0, PIECE)], skr.at[k]).wait()
    basis = interp_basis(skel[...], ranks[block_leaf(0)].astype(F32))

    for q in range(16):
        pltpu.make_async_copy(par.at[q], par.at[q], par_sem.at[q]).wait()
    count = jnp.int32(0)
    source = [jnp.int32(-1)] * 8
    for q in range(16):
        mine = owners[q] == y
        source = [jnp.where(jnp.logical_and(mine, count == k), q, source[k]) for k in range(8)]
        count = count + jnp.where(mine, 1, 0)
    for k in range(8):
        placed[0, k] = jnp.where(source[k] >= 0, par[jnp.maximum(source[k], 0)], 0.0)

    for j in range(3):
        pltpu.make_async_copy(rbuf.at[j], rbuf.at[j], rdr.at[j]).wait()
    samples = acc[0] + (rbuf[0].astype(F32) + rbuf[1].astype(F32)) + rbuf[2].astype(F32)
    interp[...] = dot3(samples, basis, ((1,), (1,)))

    @pl.when(z == y)
    def _():
        for i in range(2):
            for j in range(WAYS):
                for core in range(2):
                    @pl.when(row_target(i, j, core) != me)
                    def _():
                        row_copy(i, j, core).wait_send()

    for copy in col_sends:
        copy.wait_send()
    for half in range(2):
        for i in range(4):
            om_send(i, half).wait_send()
        for i in range(3):
            forward(2 + 2 * i, half).wait_send()
    for j in range(1, WAYS):
        piv_send(j).wait_send()
        main_send(j).wait_send()
    for k in range(3):
        skel_send(k).wait_send()
    for k in range(4):
        for g in range(4):
            if g:
                par_send(k, g).wait_send()
            else:
                @pl.when(par_dev(k) != me)
                def _():
                    par_send(k, g).wait_send()


def body(points, omega, pivots, ranks, owners):
    vmem = pl.BlockSpec(memory_space=pltpu.VMEM)
    smem = pl.BlockSpec(memory_space=pltpu.SMEM)
    dma = pltpu.SemaphoreType.DMA
    interp, placed = pl.pallas_call(
        sweep_kernel,
        name="sweep",
        out_shape=[
            jax.ShapeDtypeStruct((SLAB, RMAX), F32),
            jax.ShapeDtypeStruct((1, 8, 16, S), F32),
        ],
        in_specs=[vmem, pl.BlockSpec(memory_space=pl.ANY), vmem, smem, smem],
        out_specs=[vmem, vmem],
        scratch_shapes=[
            pltpu.VMEM((8, HALF), F32),
            pltpu.VMEM((2, 2, 8, SLAB // 2 + 128), F32),
            pltpu.VMEM((4, 8, SLAB // 2 + 128), F32),
            pltpu.VMEM((8, 8, HALF), F32),
            pltpu.VMEM((8, LEAF, S), BF),
            pltpu.VMEM((4, SLAB, DEPTH), BF),
            pltpu.VMEM((RMAX, DEPTH), BF),
            pltpu.VMEM((8, DEPTH, LEAF), BF),
            pltpu.VMEM((4, SLAB, S), F32),
            pltpu.VMEM((4, 2, PIECE, S), F32),
            pltpu.VMEM((SLAB, HALF), BF),
            pltpu.VMEM((SLAB, HALF), BF),
            pltpu.VMEM((3, SLAB, S), BF),
            pltpu.VMEM((3, SLAB, S), BF),
            pltpu.VMEM((3, 2, PIECE, S), F32),
            pltpu.VMEM((RMAX, S), F32),
            pltpu.VMEM((PIECE, S), F32),
            pltpu.VMEM((16, 16, S), F32),
            dma, dma((7,)), dma((8,)), dma((16,)), dma((4,)), dma((4, 2)), dma((8, 2)), dma((3, 2)),
            dma((3,)), dma((3,)), dma((3,)), dma((3,)), dma((3,)), dma((3,)), dma((16,)), dma((16,)),
        ],
        compiler_params=pltpu.CompilerParams(
            collective_id=0, has_side_effects=True, vmem_limit_bytes=56 * 2**20
        ),
    )(points, omega, pivots, ranks, owners)
    return interp, placed


def solution(mesh):
    placed = (P(None, "dev"), P("dev", None), P(), P(), P())
    return jax.shard_map(
        body,
        mesh=mesh,
        in_specs=placed,
        out_specs=(P(("grp", "dev"), None), P("grp", None, "dev", None)),
        check_vma=False,
    )
```

```python
import functools

import jax
import jax.numpy as jnp
from jax import lax
from jax.experimental import pallas as pl
from jax.experimental.pallas import tpu as pltpu
from jax.sharding import PartitionSpec as P

BF = jnp.bfloat16
F32 = jnp.float32
MESH = pl.DeviceIdType.MESH
HIGHEST = lax.Precision.HIGHEST
SOFTEN = 0.0001
DEPTH = 32
WAYS = 4
LEAF = 2048
SLAB = 512
S = 256
RMAX = 256
PIECE = 64
HALF = 1024
BYMXU = 640


def place():
    y = lax.axis_index("grp")
    d = lax.axis_index("dev")
    return y, d // 8, (d // 2) % 4, d % 2


def dev_of(z, x, c):
    return ((z % 4) * 4 + (x % 4)) * 2 + c


SPLIT_PAIRS = [(0, 0), (0, 1), (1, 0), (1, 1), (0, 2), (2, 0), (1, 2), (2, 1)]


def splits(value):
    high = value.astype(BF).astype(F32)
    rest = value - high
    mid = rest.astype(BF).astype(F32)
    return [high, mid, rest - mid]


def distance_rows(coords, col_side):
    n = coords.shape[1]
    row = lax.broadcasted_iota(jnp.int32, (8, n), 0)
    norm = jnp.sum(coords * coords, axis=0, keepdims=True)
    twice = coords + pltpu.roll(coords, 3, 0)
    if col_side:
        value = jnp.where(row < 6, -2.0 * twice, jnp.where(row == 6, 1.0, norm + SOFTEN))
    else:
        value = jnp.where(row < 6, twice, jnp.where(row == 6, norm, 1.0))
    parts = splits(value)
    side, varying = (1, 7) if col_side else (0, 6)
    blocks = []
    for g in range(4):
        first, second = SPLIT_PAIRS[2 * g][side], SPLIT_PAIRS[2 * g + 1][side]
        block = jnp.where(row < 3, parts[first], parts[second])
        if g < 3:
            block = jnp.where(row >= 6, jnp.where(row == varying, parts[g], 1.0), block)
        else:
            block = jnp.where(row >= 6, 0.0, block)
        blocks.append(block)
    return jnp.concatenate(blocks, axis=0), value


def centred(block):
    n = block.shape[1]
    return jnp.concatenate([block - 0.5, jnp.zeros((5, n), F32)], axis=0)


def hdot(a, b, dims):
    return lax.dot_general(a, b, (dims, ((), ())), precision=HIGHEST, preferred_element_type=F32)


def dot3(a, b, dims):
    def one(p, q):
        return lax.dot_general(p, q, (dims, ((), ())), preferred_element_type=F32)

    ah, bh = a.astype(BF), b.astype(BF)
    al, bl = (a - ah.astype(F32)).astype(BF), (b - bh.astype(F32)).astype(BF)
    return one(ah, bh) + (one(ah, bl) + one(al, bh))


def interp_basis(rows, rank):
    gram = hdot(rows, rows, ((1,), (1,)))
    squares = jnp.sum(rows * rows, axis=1, keepdims=True)
    trace = jnp.sum(squares, axis=0, keepdims=True)
    low = 0.1 * trace / rank + 1e-06
    eye = lax.broadcasted_iota(jnp.int32, (RMAX, RMAX), 0) == lax.broadcasted_iota(jnp.int32, (RMAX, RMAX), 1)
    gram = gram + jnp.where(eye, low, 0.0)
    high = low + trace
    a = 2.0 / (low + high)
    ratio = low / high
    inv = None
    for step in range(9):
        gap = (1.0 - ratio) / (1.0 + ratio)
        grow = 2.0 / (2.0 - gap * gap)
        if inv is None:
            inv = grow * (jnp.where(eye, 2.0 * a, 0.0) - a * a * gram)
        else:
            mul = dot3 if step < 7 else hdot
            prod = mul(gram, inv, ((1,), (0,)))
            inv = grow * mul(inv, jnp.where(eye, 2.0, 0.0) - prod, ((1,), (0,)))
        ratio = 1.0 - gap * gap
    return hdot(inv, rows, ((1,), (0,)))


def sweep_kernel(
    pts, om_in, pivots, ranks, owners,
    interp, placed,
    packed, outbox, inbox, cp, om, arow, apiv, bcol, rowb, ccol, acc, accp, kw0, kw1, sbuf, rbuf, prbuf, skel, red, par,
    own_sem, cps, cpr, rps, rpr, oms, omr, fws, rds, rdr, pvs, pvr, sks, skr, pas, par_sem,
):
    y, z, x, c = place()
    dirs = [(1, 0), (0, 1), (0, 3)]

    def block_chip(j):
        return (x + j) % 4, (z + 2 * (j % 2)) % 4

    def block_leaf(j):
        xr, zr = block_chip(j)
        return y * 8 + 2 * zr + xr // 2

    def to(dev, grp=None):
        return (y if grp is None else grp, dev)

    me = dev_of(z, x, c)
    own_copy = pltpu.make_async_copy(om_in, om.at[0], own_sem)
    own_copy.start()
    barrier = pltpu.get_barrier_semaphore()
    for k in range(1, 32):
        pl.semaphore_signal(barrier, inc=1, device_id=to((me + k) % 32), device_id_type=MESH)
    for gy in range(1, 4):
        for zs in range(4):
            pl.semaphore_signal(
                barrier, inc=1, device_id=to(dev_of(zs, z, x // 2), (y + gy) % 4), device_id_type=MESH
            )

    whole = centred(pts[...])
    packed[...] = whole[:, :HALF] + pltpu.roll(whole[:, HALF:], 3, 0)
    split = jnp.concatenate([*splits(whole), jnp.zeros((8, LEAF), F32)], axis=0).astype(BF)
    wanted = pivots[pl.ds(me, 1), :]
    here = lax.broadcasted_iota(jnp.int32, (LEAF, RMAX), 0) == wanted
    hit = jnp.dot(split, here.astype(BF), preferred_element_type=F32)
    picked = hit[0:8] + hit[8:16] + hit[16:24]
    first64 = lax.broadcasted_iota(jnp.int32, (8, 128), 1) < 64
    for i in range(2):
        tile = picked[:, i * 128 : (i + 1) * 128]
        other = pltpu.roll(tile, 64, 1)
        for core in range(2):
            lo = (2 * i + core) * SLAB
            outbox[i, core, :, : SLAB // 2] = whole[:, lo : lo + SLAB // 2] + pltpu.roll(
                whole[:, lo + SLAB // 2 : lo + SLAB], 3, 0
            )
            outbox[i, core, :, SLAB // 2 :] = jnp.where(first64, tile, other) if core == 0 else jnp.where(first64, other, tile)
    operand, value = distance_rows(whole, True)
    bcol[0] = operand.astype(BF)
    ccol[0] = value
    pl.semaphore_wait(barrier, 43)

    def row_copy(i, j, core):
        xr, zr = 2 * c + i, x
        return pltpu.make_async_remote_copy(
            src_ref=outbox.at[i, core], dst_ref=inbox.at[j], send_sem=rps.at[i * 8 + j * 2 + core], recv_sem=rpr.at[j],
            device_id=to(dev_of(zr - 2 * (j % 2) + 4, xr - j + 4, core)), device_id_type=MESH,
        )

    def row_target(i, j, core):
        return dev_of(x - 2 * (j % 2) + 4, 2 * c + i - j + 4, core)

    @pl.when(z == y)
    def _():
        for i in range(2):
            for j in range(WAYS):
                for core in range(2):
                    self_target = row_target(i, j, core) == me

                    @pl.when(self_target)
                    def _():
                        pltpu.make_async_copy(outbox.at[i, core], inbox.at[j], rpr.at[j]).start()

                    @pl.when(jnp.logical_not(self_target))
                    def _():
                        row_copy(i, j, core).start()

    def col_copies():
        copies = [
            pltpu.make_async_remote_copy(
                src_ref=packed, dst_ref=cp.at[1], send_sem=cps.at[0], recv_sem=cpr.at[1],
                device_id=to(dev_of(z, x, 1 - c)), device_id_type=MESH,
            )
        ]
        for i, (dx, dz) in enumerate(dirs):
            for other in range(2):
                core = c if other == 0 else 1 - c
                copies.append(
                    pltpu.make_async_remote_copy(
                        src_ref=packed, dst_ref=cp.at[2 + 2 * i + other],
                        send_sem=cps.at[1 + 2 * i + other], recv_sem=cpr.at[2 + 2 * i + other],
                        device_id=to(dev_of(z - dz + 4, x - dx + 4, core)), device_id_type=MESH,
                    )
                )
        return copies

    col_sends = col_copies()
    for copy in col_sends:
        copy.start()

    def om_send(i, half):
        rows = pl.ds(half * HALF, HALF)
        if i == 0:
            slot, dev = 1, dev_of(z, x, 1 - c)
        else:
            dx, dz = dirs[i - 1]
            slot, dev = 2 * i, dev_of(z - dz + 4, x - dx + 4, c)
        return pltpu.make_async_remote_copy(
            src_ref=om_in.at[rows], dst_ref=om.at[slot, rows], send_sem=oms.at[i, half],
            recv_sem=omr.at[slot, half], device_id=to(dev), device_id_type=MESH,
        )

    for half in range(2):
        for i in range(4):
            om_send(i, half).start()

    def forward(slot, half):
        rows = pl.ds(half * HALF, HALF)
        return pltpu.make_async_remote_copy(
            src_ref=om.at[slot, rows], dst_ref=om.at[slot + 1, rows], send_sem=fws.at[slot // 2 - 1, half],
            recv_sem=omr.at[slot + 1, half], device_id=to(dev_of(z, x, 1 - c)), device_id_type=MESH,
        )

    def om_arrived(slot, half):
        rows = pl.ds(half * HALF, HALF)
        pltpu.make_async_copy(om.at[slot, rows], om.at[slot, rows], omr.at[slot, half]).wait()

    xyz = lax.broadcasted_iota(jnp.int32, (8, 1), 0) < 3

    def build_col(slot):
        pltpu.make_async_copy(cp.at[slot], cp.at[slot], cpr.at[slot]).wait()
        both = cp[slot]
        for h in range(2):
            coords = jnp.where(xyz, both if h == 0 else pltpu.roll(both, 5, 0), 0.0)
            operand, value = distance_rows(coords, True)
            bcol[slot, :, h * HALF : (h + 1) * HALF] = operand.astype(BF)
            ccol[slot, :, h * HALF : (h + 1) * HALF] = value

    pick = [None, None]
    for j in range(WAYS):
        pltpu.make_async_copy(inbox.at[j], inbox.at[j], rpr.at[j]).wait()
        got = inbox[j]
        pair = got[:, : SLAB // 2]
        coords = jnp.concatenate([jnp.where(xyz, pair, 0.0), jnp.where(xyz, pltpu.roll(pair, 5, 0), 0.0)], axis=1)
        operand = distance_rows(coords, False)[0].T.astype(BF)
        arow[j * SLAB : (j + 1) * SLAB] = operand
        for k in range(4):
            chosen = (6, 14, 22) if k == 3 else (k, 8 + k, 19 + k)
            depth = lax.broadcasted_iota(jnp.int32, (DEPTH, 128), 0)
            ones = jnp.where(depth == chosen[0], 1.0, jnp.where(depth == chosen[1], 1.0, jnp.where(depth == chosen[2], 1.0, 0.0)))
            rowb[k, j * SLAB : (j + 1) * SLAB] = jnp.dot(operand, ones.astype(BF), preferred_element_type=F32)
        points = got[:, SLAB // 2 :]
        pick[j // 2] = points if j % 2 == 0 else jnp.where(first64, pick[j // 2], points)
    for t in range(2):
        apiv[t * 128 : (t + 1) * 128] = distance_rows(pick[t], False)[0].T.astype(BF)
    build_col(1)
    own_copy.wait()

    acc[...] = jnp.zeros_like(acc)
    accp[...] = jnp.zeros_like(accp)

    def nth(i):
        k = (i - 4) % 6
        late = i >= 4
        slot = jnp.where(late, jnp.where(k < 3, 2 + 2 * k, 3 + 2 * (k - 3)), i // 2)
        half = jnp.where(late, (i - 4) // 6, i % 2)
        return slot, half

    def slot_leaf(slot):
        pair = slot // 2
        xq = jnp.where(pair == 1, x + 1, x) % 4
        zq = (z + jnp.where(pair == 2, 1, jnp.where(pair == 3, 3, 0))) % 4
        cq = jnp.where(slot % 2 == 0, c, 1 - c)
        return dev_of(zq, xq, cq)

    def gen_piv(slot, half, kb):
        cols = pl.ds(pl.multiple_of(half * HALF, HALF), HALF)
        dist = jnp.dot(apiv[...], bcol[slot, :, cols], preferred_element_type=F32)
        kb[...] = lax.rsqrt(dist).astype(BF)

    def gen(start, n, slot, half, kb):
        base = pl.multiple_of(half * HALF, HALF)
        rows = arow[pl.ds(pl.multiple_of(start, SLAB), n), :]
        dist = jnp.dot(rows, bcol[slot, :, pl.ds(base, BYMXU)], preferred_element_type=F32)
        kb[:, :BYMXU] = lax.rsqrt(dist).astype(BF)
        for r in range(0, n, 8):
            at = pl.ds(pl.multiple_of(start + r, 8), 8)
            rx, ry, rz, rn = [rowb[k, at, :] for k in range(4)]
            for t in range(BYMXU, HALF, 128):
                cols = pl.ds(pl.multiple_of(base + t, 128), 128)
                cx, cy, cz, cn = [ccol[slot, k : k + 1, cols] for k in (0, 1, 2, 7)]
                dist = ((rn + cn) + rx * cx) + (ry * cy + rz * cz)
                kb[r : r + 8, t : t + 128] = lax.rsqrt(dist).astype(BF)

    def product(slot, half, kb):
        rows = pl.ds(pl.multiple_of(half * HALF, HALF), HALF)
        return jnp.dot(kb[...], om[slot, rows, :], preferred_element_type=F32)

    def use_main(slot, half, j, kb, blocks):
        got = product(slot, half, kb)
        for e in range(blocks):
            keep = jnp.where(slot_leaf(slot) == block_leaf(j + e), 0.0, 1.0).astype(F32)
            acc[pl.ds(pl.multiple_of((j + e) * SLAB, SLAB), SLAB), :] += keep * got[e * SLAB : (e + 1) * SLAB]

    def ready(i):
        slot, half = nth(i)

        @pl.when(i >= 2)
        def _():
            om_arrived(slot, half)

        @pl.when(jnp.logical_and(slot >= 2, slot % 2 == 0))
        def _():
            forward(slot, half).start()

    gen(0, 2 * SLAB, 0, 0, kw0)

    @pl.loop(0, 10)
    def _(i):
        slot, half = nth(i)
        ready(i)

        @pl.when(jnp.logical_and(i >= 3, i < 9))
        def _():
            build_col(nth(i + 1)[0])

        @pl.when(i == 8)
        def _():
            for late in range(10, 13):
                ready(jnp.int32(late))

        gen(2 * SLAB, 2 * SLAB, slot, half, kw1)
        use_main(slot, half, 0, kw0, 2)
        nslot, nhalf = nth(jnp.minimum(i + 1, 9))
        gen(0, 2 * SLAB, nslot, nhalf, kw0)
        use_main(slot, half, 2, kw1, 2)

    kp0, kp1 = kw0.at[pl.ds(0, RMAX)], kw1.at[pl.ds(0, RMAX)]
    kb0, kb1 = kw0.at[pl.ds(0, SLAB)], kw1.at[pl.ds(0, SLAB)]

    def use_piv(slot, half, kb):
        got = product(slot, half, kb)
        for j in range(WAYS):
            own = slot_leaf(slot) == block_leaf(j)
            sib = dev_of(slot_leaf(slot) // 8, (slot_leaf(slot) // 2) % 4, 1 - slot_leaf(slot) % 2) == block_leaf(j)
            part = got[j * PIECE : (j + 1) * PIECE]
            accp[j, 0] += jnp.where(jnp.logical_or(own, sib), 0.0, 1.0).astype(F32) * part
            accp[j, 1] += jnp.where(sib, 1.0, 0.0).astype(F32) * part

    gen_piv(0, 0, kp0)

    @pl.loop(0, 8)
    def _(t):
        @pl.when(t >= 6)
        def _():
            for e in range(2):
                @pl.when(2 * t + e >= 13)
                def _():
                    slot, half = nth(2 * t + e)
                    om_arrived(slot, half)

        slot, half = nth(2 * t)
        slot1, half1 = nth(2 * t + 1)
        gen_piv(slot1, half1, kp1)
        use_piv(slot, half, kp0)
        slot2, half2 = nth(jnp.minimum(2 * t + 2, 15))
        gen_piv(slot2, half2, kp0)
        use_piv(slot1, half1, kp1)

    def piv_send(j):
        xr, zr = block_chip(j)
        return pltpu.make_async_remote_copy(
            src_ref=accp.at[j], dst_ref=prbuf.at[j - 1], send_sem=pvs.at[j - 1], recv_sem=pvr.at[j - 1],
            device_id=to(dev_of(zr, xr, c)), device_id_type=MESH,
        )

    for j in range(1, WAYS):
        piv_send(j).start()

    def main_send(j):
        xr, zr = block_chip(j)
        return pltpu.make_async_remote_copy(
            src_ref=sbuf.at[j - 1], dst_ref=rbuf.at[j - 1], send_sem=rds.at[j - 1], recv_sem=rdr.at[j - 1],
            device_id=to(dev_of(zr, xr, c)), device_id_type=MESH,
        )

    piece = 2 * (x % 2) + c
    piece_rows = pl.ds(pl.multiple_of(piece * PIECE, PIECE), PIECE)

    def skel_send(k):
        xs = x if k == 0 else x + 1 - 2 * (x % 2)
        core = 1 - c if k != 1 else c
        return pltpu.make_async_remote_copy(
            src_ref=skel.at[piece_rows], dst_ref=skel.at[piece_rows], send_sem=sks.at[k], recv_sem=skr.at[k],
            device_id=to(dev_of(z, xs, core)), device_id_type=MESH,
        )

    def par_dev(k):
        return dev_of(x, 2 * c + k // 2, k % 2)

    def par_send(k, g):
        return pltpu.make_async_remote_copy(
            src_ref=red.at[pl.ds(k * 16, 16)], dst_ref=par.at[4 * y + z], send_sem=pas.at[4 * g + k],
            recv_sem=par_sem.at[4 * y + z], device_id=to(par_dev(k), (y + g) % 4), device_id_type=MESH,
        )

    def finish_pivots():
        for j in range(3):
            pltpu.make_async_copy(prbuf.at[j], prbuf.at[j], pvr.at[j]).wait()
        total = accp[0] + prbuf[0] + prbuf[1] + prbuf[2]
        ids = lax.broadcasted_iota(jnp.int32, (PIECE, S), 0) + piece * PIECE
        live = ids < ranks[block_leaf(0)]
        skel[piece_rows, :] = jnp.where(live, total[0] + total[1], 0.0)
        red[...] = jnp.where(live, total[0], 0.0)
        for k in range(3):
            skel_send(k).start()
        for k in range(4):
            for g in range(4):
                if g:
                    par_send(k, g).start()
                else:
                    self_target = par_dev(k) == me

                    @pl.when(self_target)
                    def _():
                        pltpu.make_async_copy(
                            red.at[pl.ds(k * 16, 16)], par.at[4 * y + z], par_sem.at[4 * y + z]
                        ).start()

                    @pl.when(jnp.logical_not(self_target))
                    def _():
                        par_send(k, g).start()

    def turn(t):
        k = t // 3
        return jnp.where(k < 2, 1 + 2 * k, 2 * (3 - k))

    gen(SLAB, SLAB, 2, 1, kb0)

    @pl.loop(0, 12)
    def _(t):
        j = turn(t)
        i = 10 + 2 * (t % 3)

        @pl.when(t == 4)
        def _():
            finish_pivots()

        slot, half = nth(i)
        slot1, half1 = nth(i + 1)
        gen(j * SLAB, SLAB, slot1, half1, kb1)
        use_main(slot, half, j, kb0, 1)
        nxt = jnp.minimum(t + 1, 11)
        slot2, half2 = nth(10 + 2 * (nxt % 3))
        gen(turn(nxt) * SLAB, SLAB, slot2, half2, kb0)
        use_main(slot1, half1, j, kb1, 1)
        for jj, last in ((1, 2), (3, 5), (2, 8)):
            @pl.when(t == last)
            def _():
                sbuf[jj - 1] = acc[jj * SLAB : (jj + 1) * SLAB].astype(BF)
                main_send(jj).start()

    for k in range(3):
        pltpu.make_async_copy(skel.at[pl.ds(0, PIECE)], skel.at[pl.ds(0, PIECE)], skr.at[k]).wait()
    basis = interp_basis(skel[...], ranks[block_leaf(0)].astype(F32))

    for q in range(16):
        pltpu.make_async_copy(par.at[q], par.at[q], par_sem.at[q]).wait()
    count = jnp.int32(0)
    source = [jnp.int32(-1)] * 8
    for q in range(16):
        mine = owners[q] == y
        source = [jnp.where(jnp.logical_and(mine, count == k), q, source[k]) for k in range(8)]
        count = count + jnp.where(mine, 1, 0)
    for k in range(8):
        placed[0, k] = jnp.where(source[k] >= 0, par[jnp.maximum(source[k], 0)], 0.0)

    for j in range(3):
        pltpu.make_async_copy(rbuf.at[j], rbuf.at[j], rdr.at[j]).wait()
    samples = acc[:SLAB] + (rbuf[0].astype(F32) + rbuf[1].astype(F32)) + rbuf[2].astype(F32)
    interp[...] = dot3(samples, basis, ((1,), (1,)))

    @pl.when(z == y)
    def _():
        for i in range(2):
            for j in range(WAYS):
                for core in range(2):
                    @pl.when(row_target(i, j, core) != me)
                    def _():
                        row_copy(i, j, core).wait_send()

    for copy in col_sends:
        copy.wait_send()
    for half in range(2):
        for i in range(4):
            om_send(i, half).wait_send()
        for i in range(3):
            forward(2 + 2 * i, half).wait_send()
    for j in range(1, WAYS):
        piv_send(j).wait_send()
        main_send(j).wait_send()
    for k in range(3):
        skel_send(k).wait_send()
    for k in range(4):
        for g in range(4):
            if g:
                par_send(k, g).wait_send()
            else:
                @pl.when(par_dev(k) != me)
                def _():
                    par_send(k, g).wait_send()


def body(points, omega, pivots, ranks, owners):
    vmem = pl.BlockSpec(memory_space=pltpu.VMEM)
    smem = pl.BlockSpec(memory_space=pltpu.SMEM)
    dma = pltpu.SemaphoreType.DMA
    interp, placed = pl.pallas_call(
        sweep_kernel,
        name="sweep",
        out_shape=[
            jax.ShapeDtypeStruct((SLAB, RMAX), F32),
            jax.ShapeDtypeStruct((1, 8, 16, S), F32),
        ],
        in_specs=[vmem, pl.BlockSpec(memory_space=pl.ANY), vmem, smem, smem],
        out_specs=[vmem, vmem],
        scratch_shapes=[
            pltpu.VMEM((8, HALF), F32),
            pltpu.VMEM((2, 2, 8, SLAB // 2 + 128), F32),
            pltpu.VMEM((4, 8, SLAB // 2 + 128), F32),
            pltpu.VMEM((8, 8, HALF), F32),
            pltpu.VMEM((8, LEAF, S), BF),
            pltpu.VMEM((4 * SLAB, DEPTH), BF),
            pltpu.VMEM((RMAX, DEPTH), BF),
            pltpu.VMEM((8, DEPTH, LEAF), BF),
            pltpu.VMEM((4, 4 * SLAB, 128), F32),
            pltpu.VMEM((8, 8, LEAF), F32),
            pltpu.VMEM((4 * SLAB, S), F32),
            pltpu.VMEM((4, 2, PIECE, S), F32),
            pltpu.VMEM((2 * SLAB, HALF), BF),
            pltpu.VMEM((2 * SLAB, HALF), BF),
            pltpu.VMEM((3, SLAB, S), BF),
            pltpu.VMEM((3, SLAB, S), BF),
            pltpu.VMEM((3, 2, PIECE, S), F32),
            pltpu.VMEM((RMAX, S), F32),
            pltpu.VMEM((PIECE, S), F32),
            pltpu.VMEM((16, 16, S), F32),
            dma, dma((7,)), dma((8,)), dma((16,)), dma((4,)), dma((4, 2)), dma((8, 2)), dma((3, 2)),
            dma((3,)), dma((3,)), dma((3,)), dma((3,)), dma((3,)), dma((3,)), dma((16,)), dma((16,)),
        ],
        compiler_params=pltpu.CompilerParams(
            collective_id=0, has_side_effects=True, vmem_limit_bytes=56 * 2**20
        ),
    )(points, omega, pivots, ranks, owners)
    return interp, placed


def solution(mesh):
    placed = (P(None, "dev"), P("dev", None), P(), P(), P())
    return jax.shard_map(
        body,
        mesh=mesh,
        in_specs=placed,
        out_specs=(P(("grp", "dev"), None), P("grp", None, "dev", None)),
        check_vma=False,
    )
```

```python
import functools

import jax
import jax.numpy as jnp
from jax import lax
from jax.experimental import pallas as pl
from jax.experimental.pallas import tpu as pltpu
from jax.sharding import PartitionSpec as P

BF = jnp.bfloat16
F32 = jnp.float32
MESH = pl.DeviceIdType.MESH
HIGHEST = lax.Precision.HIGHEST
SOFTEN = 0.0001
DEPTH = 32
WAYS = 4
LEAF = 2048
SLAB = 512
S = 256
RMAX = 256
PIECE = 64
HALF = 1024
BYMXU = 640


def place():
    y = lax.axis_index("grp")
    d = lax.axis_index("dev")
    return y, d // 8, (d // 2) % 4, d % 2


def dev_of(z, x, c):
    return ((z % 4) * 4 + (x % 4)) * 2 + c


SPLIT_PAIRS = [(0, 0), (0, 1), (1, 0), (1, 1), (0, 2), (2, 0), (1, 2), (2, 1)]


def splits(value):
    high = value.astype(BF).astype(F32)
    rest = value - high
    mid = rest.astype(BF).astype(F32)
    return [high, mid, rest - mid]


def distance_rows(coords, col_side):
    n = coords.shape[1]
    row = lax.broadcasted_iota(jnp.int32, (8, n), 0)
    norm = jnp.sum(coords * coords, axis=0, keepdims=True)
    twice = coords + pltpu.roll(coords, 3, 0)
    if col_side:
        value = jnp.where(row < 6, -2.0 * twice, jnp.where(row == 6, 1.0, norm + SOFTEN))
    else:
        value = jnp.where(row < 6, twice, jnp.where(row == 6, norm, 1.0))
    parts = splits(value)
    side, varying = (1, 7) if col_side else (0, 6)
    blocks = []
    for g in range(4):
        first, second = SPLIT_PAIRS[2 * g][side], SPLIT_PAIRS[2 * g + 1][side]
        block = jnp.where(row < 3, parts[first], parts[second])
        if g < 3:
            block = jnp.where(row >= 6, jnp.where(row == varying, parts[g], 1.0), block)
        else:
            block = jnp.where(row >= 6, 0.0, block)
        blocks.append(block)
    return jnp.concatenate(blocks, axis=0), value


def centred(block):
    n = block.shape[1]
    return jnp.concatenate([block - 0.5, jnp.zeros((5, n), F32)], axis=0)


def hdot(a, b, dims):
    return lax.dot_general(a, b, (dims, ((), ())), precision=HIGHEST, preferred_element_type=F32)


def dot3(a, b, dims):
    def one(p, q):
        return lax.dot_general(p, q, (dims, ((), ())), preferred_element_type=F32)

    ah, bh = a.astype(BF), b.astype(BF)
    al, bl = (a - ah.astype(F32)).astype(BF), (b - bh.astype(F32)).astype(BF)
    return one(ah, bh) + (one(ah, bl) + one(al, bh))


def interp_basis(rows, rank):
    gram = hdot(rows, rows, ((1,), (1,)))
    squares = jnp.sum(rows * rows, axis=1, keepdims=True)
    trace = jnp.sum(squares, axis=0, keepdims=True)
    low = 0.1 * trace / rank + 1e-06
    eye = lax.broadcasted_iota(jnp.int32, (RMAX, RMAX), 0) == lax.broadcasted_iota(jnp.int32, (RMAX, RMAX), 1)
    gram = gram + jnp.where(eye, low, 0.0)
    high = low + trace
    a = 2.0 / (low + high)
    ratio = low / high
    inv = None
    for step in range(9):
        gap = (1.0 - ratio) / (1.0 + ratio)
        grow = 2.0 / (2.0 - gap * gap)
        if inv is None:
            inv = grow * (jnp.where(eye, 2.0 * a, 0.0) - a * a * gram)
        else:
            mul = dot3 if step < 7 else hdot
            prod = mul(gram, inv, ((1,), (0,)))
            inv = grow * mul(inv, jnp.where(eye, 2.0, 0.0) - prod, ((1,), (0,)))
        ratio = 1.0 - gap * gap
    return hdot(inv, rows, ((1,), (0,)))


def sweep_kernel(
    pts, om_in, pivots, ranks, owners,
    interp, placed,
    packed, outbox, inbox, cp, om, arow, apiv, bcol, rowb, ccol, acc, accp, kw0, kw1, sbuf, rbuf, prbuf, skel, red, par,
    own_sem, cps, cpr, rps, rpr, oms, omr, fws, rds, rdr, pvs, pvr, sks, skr, pas, par_sem,
):
    y, z, x, c = place()
    dirs = [(1, 0), (0, 1), (0, 3)]

    def block_chip(j):
        return (x + j) % 4, (z + 2 * (j % 2)) % 4

    def block_leaf(j):
        xr, zr = block_chip(j)
        return y * 8 + 2 * zr + xr // 2

    def to(dev, grp=None):
        return (y if grp is None else grp, dev)

    me = dev_of(z, x, c)
    own_copy = pltpu.make_async_copy(om_in, om.at[0], own_sem)
    own_copy.start()
    barrier = pltpu.get_barrier_semaphore()
    for k in range(1, 32):
        pl.semaphore_signal(barrier, inc=1, device_id=to((me + k) % 32), device_id_type=MESH)
    for gy in range(1, 4):
        for zs in range(4):
            pl.semaphore_signal(
                barrier, inc=1, device_id=to(dev_of(zs, z, x // 2), (y + gy) % 4), device_id_type=MESH
            )

    whole = centred(pts[...])
    packed[...] = whole[:, :HALF] + pltpu.roll(whole[:, HALF:], 3, 0)
    split = jnp.concatenate([*splits(whole), jnp.zeros((8, LEAF), F32)], axis=0).astype(BF)
    wanted = pivots[pl.ds(me, 1), :]
    here = lax.broadcasted_iota(jnp.int32, (LEAF, RMAX), 0) == wanted
    hit = jnp.dot(split, here.astype(BF), preferred_element_type=F32)
    picked = hit[0:8] + hit[8:16] + hit[16:24]
    first64 = lax.broadcasted_iota(jnp.int32, (8, 128), 1) < 64
    for i in range(2):
        tile = picked[:, i * 128 : (i + 1) * 128]
        other = pltpu.roll(tile, 64, 1)
        for core in range(2):
            lo = (2 * i + core) * SLAB
            outbox[i, core, :, : SLAB // 2] = whole[:, lo : lo + SLAB // 2] + pltpu.roll(
                whole[:, lo + SLAB // 2 : lo + SLAB], 3, 0
            )
            outbox[i, core, :, SLAB // 2 :] = jnp.where(first64, tile, other) if core == 0 else jnp.where(first64, other, tile)
    operand, value = distance_rows(whole, True)
    bcol[0] = operand.astype(BF)
    ccol[0] = value
    pl.semaphore_wait(barrier, 43)

    def row_copy(i, j, core):
        xr, zr = 2 * c + i, x
        return pltpu.make_async_remote_copy(
            src_ref=outbox.at[i, core], dst_ref=inbox.at[j], send_sem=rps.at[i * 8 + j * 2 + core], recv_sem=rpr.at[j],
            device_id=to(dev_of(zr - 2 * (j % 2) + 4, xr - j + 4, core)), device_id_type=MESH,
        )

    def row_target(i, j, core):
        return dev_of(x - 2 * (j % 2) + 4, 2 * c + i - j + 4, core)

    @pl.when(z == y)
    def _():
        for i in range(2):
            for j in range(WAYS):
                for core in range(2):
                    self_target = row_target(i, j, core) == me

                    @pl.when(self_target)
                    def _():
                        pltpu.make_async_copy(outbox.at[i, core], inbox.at[j], rpr.at[j]).start()

                    @pl.when(jnp.logical_not(self_target))
                    def _():
                        row_copy(i, j, core).start()

    def col_copies():
        copies = [
            pltpu.make_async_remote_copy(
                src_ref=packed, dst_ref=cp.at[1], send_sem=cps.at[0], recv_sem=cpr.at[1],
                device_id=to(dev_of(z, x, 1 - c)), device_id_type=MESH,
            )
        ]
        for i, (dx, dz) in enumerate(dirs):
            for other in range(2):
                core = c if other == 0 else 1 - c
                copies.append(
                    pltpu.make_async_remote_copy(
                        src_ref=packed, dst_ref=cp.at[2 + 2 * i + other],
                        send_sem=cps.at[1 + 2 * i + other], recv_sem=cpr.at[2 + 2 * i + other],
                        device_id=to(dev_of(z - dz + 4, x - dx + 4, core)), device_id_type=MESH,
                    )
                )
        return copies

    col_sends = col_copies()
    for copy in col_sends:
        copy.start()

    def om_send(i, half):
        rows = pl.ds(half * HALF, HALF)
        if i == 0:
            slot, dev = 1, dev_of(z, x, 1 - c)
        else:
            dx, dz = dirs[i - 1]
            slot, dev = 2 * i, dev_of(z - dz + 4, x - dx + 4, c)
        return pltpu.make_async_remote_copy(
            src_ref=om_in.at[rows], dst_ref=om.at[slot, rows], send_sem=oms.at[i, half],
            recv_sem=omr.at[slot, half], device_id=to(dev), device_id_type=MESH,
        )

    for half in range(2):
        for i in range(4):
            om_send(i, half).start()

    def forward(slot, half):
        rows = pl.ds(half * HALF, HALF)
        return pltpu.make_async_remote_copy(
            src_ref=om.at[slot, rows], dst_ref=om.at[slot + 1, rows], send_sem=fws.at[slot // 2 - 1, half],
            recv_sem=omr.at[slot + 1, half], device_id=to(dev_of(z, x, 1 - c)), device_id_type=MESH,
        )

    def om_arrived(slot, half):
        rows = pl.ds(half * HALF, HALF)
        pltpu.make_async_copy(om.at[slot, rows], om.at[slot, rows], omr.at[slot, half]).wait()

    xyz = lax.broadcasted_iota(jnp.int32, (8, 1), 0) < 3

    def build_col(slot):
        pltpu.make_async_copy(cp.at[slot], cp.at[slot], cpr.at[slot]).wait()
        both = cp[slot]
        for h in range(2):
            coords = jnp.where(xyz, both if h == 0 else pltpu.roll(both, 5, 0), 0.0)
            operand, value = distance_rows(coords, True)
            bcol[slot, :, h * HALF : (h + 1) * HALF] = operand.astype(BF)
            ccol[slot, :, h * HALF : (h + 1) * HALF] = value

    pick = [None, None]
    for j in range(WAYS):
        pltpu.make_async_copy(inbox.at[j], inbox.at[j], rpr.at[j]).wait()
        got = inbox[j]
        pair = got[:, : SLAB // 2]
        coords = jnp.concatenate([jnp.where(xyz, pair, 0.0), jnp.where(xyz, pltpu.roll(pair, 5, 0), 0.0)], axis=1)
        operand = distance_rows(coords, False)[0].T.astype(BF)
        arow[j * SLAB : (j + 1) * SLAB] = operand
        for k in range(4):
            chosen = (6, 14, 22) if k == 3 else (k, 8 + k, 19 + k)
            depth = lax.broadcasted_iota(jnp.int32, (DEPTH, 128), 0)
            ones = jnp.where(depth == chosen[0], 1.0, jnp.where(depth == chosen[1], 1.0, jnp.where(depth == chosen[2], 1.0, 0.0)))
            rowb[k, j * SLAB : (j + 1) * SLAB] = jnp.dot(operand, ones.astype(BF), preferred_element_type=F32)
        points = got[:, SLAB // 2 :]
        pick[j // 2] = points if j % 2 == 0 else jnp.where(first64, pick[j // 2], points)
    for t in range(2):
        apiv[t * 128 : (t + 1) * 128] = distance_rows(pick[t], False)[0].T.astype(BF)
    build_col(1)
    own_copy.wait()

    acc[...] = jnp.zeros_like(acc)
    accp[...] = jnp.zeros_like(accp)

    def nth(i):
        k = (i - 4) % 6
        late = i >= 4
        slot = jnp.where(late, jnp.where(k < 3, 2 + 2 * k, 3 + 2 * (k - 3)), i // 2)
        half = jnp.where(late, (i - 4) // 6, i % 2)
        return slot, half

    def slot_leaf(slot):
        pair = slot // 2
        xq = jnp.where(pair == 1, x + 1, x) % 4
        zq = (z + jnp.where(pair == 2, 1, jnp.where(pair == 3, 3, 0))) % 4
        cq = jnp.where(slot % 2 == 0, c, 1 - c)
        return dev_of(zq, xq, cq)

    def gen_piv(slot, half, kb):
        cols = pl.ds(pl.multiple_of(half * HALF, HALF), HALF)
        dist = jnp.dot(apiv[...], bcol[slot, :, cols], preferred_element_type=F32)
        kb[...] = lax.rsqrt(dist).astype(BF)

    def gen(start, n, slot, half, kb):
        base = pl.multiple_of(half * HALF, HALF)
        rows = arow[pl.ds(pl.multiple_of(start, SLAB), n), :]
        dist = jnp.dot(rows, bcol[slot, :, pl.ds(base, BYMXU)], preferred_element_type=F32)
        kb[:, :BYMXU] = lax.rsqrt(dist).astype(BF)
        for r in range(0, n, 8):
            at = pl.ds(pl.multiple_of(start + r, 8), 8)
            rx, ry, rz, rn = [rowb[k, at, :] for k in range(4)]
            for t in range(BYMXU, HALF, 128):
                cols = pl.ds(pl.multiple_of(base + t, 128), 128)
                cx, cy, cz, cn = [ccol[slot, k : k + 1, cols] for k in (0, 1, 2, 7)]
                dist = ((rn + cn) + rx * cx) + (ry * cy + rz * cz)
                kb[r : r + 8, t : t + 128] = lax.rsqrt(dist).astype(BF)

    def product(slot, half, kb):
        rows = pl.ds(pl.multiple_of(half * HALF, HALF), HALF)
        return jnp.dot(kb[...], om[slot, rows, :], preferred_element_type=F32)

    def use_main(slot, half, j, kb, blocks):
        got = product(slot, half, kb)
        for e in range(blocks):
            keep = jnp.where(slot_leaf(slot) == block_leaf(j + e), 0.0, 1.0).astype(F32)
            acc[pl.ds(pl.multiple_of((j + e) * SLAB, SLAB), SLAB), :] += keep * got[e * SLAB : (e + 1) * SLAB]

    def ready(i):
        slot, half = nth(i)

        @pl.when(i >= 2)
        def _():
            om_arrived(slot, half)

        @pl.when(jnp.logical_and(slot >= 2, slot % 2 == 0))
        def _():
            forward(slot, half).start()

    gen(0, 2 * SLAB, 0, 0, kw0)

    @pl.loop(0, 10)
    def _(i):
        slot, half = nth(i)
        ready(i)

        @pl.when(jnp.logical_and(i >= 3, i < 9))
        def _():
            build_col(nth(i + 1)[0])

        @pl.when(i == 8)
        def _():
            for late in range(10, 13):
                ready(jnp.int32(late))

        gen(2 * SLAB, 2 * SLAB, slot, half, kw1)
        use_main(slot, half, 0, kw0, 2)
        nslot, nhalf = nth(jnp.minimum(i + 1, 9))
        gen(0, 2 * SLAB, nslot, nhalf, kw0)
        use_main(slot, half, 2, kw1, 2)

    kp0, kp1 = kw0.at[pl.ds(0, RMAX)], kw1.at[pl.ds(0, RMAX)]
    kb0, kb1 = kw0.at[pl.ds(0, SLAB)], kw1.at[pl.ds(0, SLAB)]

    def use_piv(slot, half, kb):
        got = product(slot, half, kb)
        for j in range(WAYS):
            own = slot_leaf(slot) == block_leaf(j)
            sib = dev_of(slot_leaf(slot) // 8, (slot_leaf(slot) // 2) % 4, 1 - slot_leaf(slot) % 2) == block_leaf(j)
            part = got[j * PIECE : (j + 1) * PIECE]
            accp[j, 0] += jnp.where(jnp.logical_or(own, sib), 0.0, 1.0).astype(F32) * part
            accp[j, 1] += jnp.where(sib, 1.0, 0.0).astype(F32) * part

    gen_piv(0, 0, kp0)

    @pl.loop(0, 8)
    def _(t):
        @pl.when(t >= 6)
        def _():
            for e in range(2):
                @pl.when(2 * t + e >= 13)
                def _():
                    slot, half = nth(2 * t + e)
                    om_arrived(slot, half)

        slot, half = nth(2 * t)
        slot1, half1 = nth(2 * t + 1)
        gen_piv(slot1, half1, kp1)
        use_piv(slot, half, kp0)
        slot2, half2 = nth(jnp.minimum(2 * t + 2, 15))
        gen_piv(slot2, half2, kp0)
        use_piv(slot1, half1, kp1)

    def piv_send(j, part):
        xr, zr = block_chip(j)
        return pltpu.make_async_remote_copy(
            src_ref=accp.at[j, part], dst_ref=prbuf.at[j - 1, part], send_sem=pvs.at[j - 1, part],
            recv_sem=pvr.at[j - 1, part], device_id=to(dev_of(zr, xr, c)), device_id_type=MESH,
        )

    def has_sibling(px, pz, j):
        dx, dz = (pz + 2 * (j % 2) - px + 4) % 4, (y - pz + 4) % 4
        return jnp.logical_or(
            jnp.logical_and(dz == 0, dx <= 1), jnp.logical_and(dx == 0, jnp.logical_or(dz == 1, dz == 3))
        )

    for j in range(1, WAYS):
        piv_send(j, 0).start()

        @pl.when(has_sibling(x, z, j))
        def _():
            piv_send(j, 1).start()

    def main_send(j):
        xr, zr = block_chip(j)
        return pltpu.make_async_remote_copy(
            src_ref=sbuf.at[j - 1], dst_ref=rbuf.at[j - 1], send_sem=rds.at[j - 1], recv_sem=rdr.at[j - 1],
            device_id=to(dev_of(zr, xr, c)), device_id_type=MESH,
        )

    piece = 2 * (x % 2) + c
    piece_rows = pl.ds(pl.multiple_of(piece * PIECE, PIECE), PIECE)

    def skel_send(k):
        xs = x if k == 0 else x + 1 - 2 * (x % 2)
        core = 1 - c if k != 1 else c
        return pltpu.make_async_remote_copy(
            src_ref=skel.at[piece_rows], dst_ref=skel.at[piece_rows], send_sem=sks.at[k], recv_sem=skr.at[k],
            device_id=to(dev_of(z, xs, core)), device_id_type=MESH,
        )

    def par_dev(k):
        return dev_of(x, 2 * c + k // 2, k % 2)

    def par_send(k, g):
        return pltpu.make_async_remote_copy(
            src_ref=red.at[pl.ds(k * 16, 16)], dst_ref=par.at[4 * y + z], send_sem=pas.at[4 * g + k],
            recv_sem=par_sem.at[4 * y + z], device_id=to(par_dev(k), (y + g) % 4), device_id_type=MESH,
        )

    def finish_pivots():
        corr = accp[0, 1]
        for j in range(1, WAYS):
            sent = has_sibling((x - j + 4) % 4, (z - 2 * (j % 2) + 4) % 4, j)
            pltpu.make_async_copy(prbuf.at[j - 1, 0], prbuf.at[j - 1, 0], pvr.at[j - 1, 0]).wait()

            @pl.when(sent)
            def _():
                pltpu.make_async_copy(prbuf.at[j - 1, 1], prbuf.at[j - 1, 1], pvr.at[j - 1, 1]).wait()

            @pl.when(jnp.logical_not(sent))
            def _():
                prbuf[j - 1, 1] = jnp.zeros((PIECE, S), F32)

            corr = corr + prbuf[j - 1, 1]
        rest = accp[0, 0] + prbuf[0, 0] + prbuf[1, 0] + prbuf[2, 0]
        ids = lax.broadcasted_iota(jnp.int32, (PIECE, S), 0) + piece * PIECE
        live = ids < ranks[block_leaf(0)]
        skel[piece_rows, :] = jnp.where(live, rest + corr, 0.0)
        red[...] = jnp.where(live, rest, 0.0)
        for k in range(3):
            skel_send(k).start()
        for k in range(4):
            for g in range(4):
                if g:
                    par_send(k, g).start()
                else:
                    self_target = par_dev(k) == me

                    @pl.when(self_target)
                    def _():
                        pltpu.make_async_copy(
                            red.at[pl.ds(k * 16, 16)], par.at[4 * y + z], par_sem.at[4 * y + z]
                        ).start()

                    @pl.when(jnp.logical_not(self_target))
                    def _():
                        par_send(k, g).start()

    def turn(t):
        k = t // 3
        return jnp.where(k < 2, 1 + 2 * k, 2 * (3 - k))

    gen(SLAB, SLAB, 2, 1, kb0)

    @pl.loop(0, 12)
    def _(t):
        j = turn(t)
        i = 10 + 2 * (t % 3)

        @pl.when(t == 4)
        def _():
            finish_pivots()

        slot, half = nth(i)
        slot1, half1 = nth(i + 1)
        gen(j * SLAB, SLAB, slot1, half1, kb1)
        use_main(slot, half, j, kb0, 1)
        nxt = jnp.minimum(t + 1, 11)
        slot2, half2 = nth(10 + 2 * (nxt % 3))
        gen(turn(nxt) * SLAB, SLAB, slot2, half2, kb0)
        use_main(slot1, half1, j, kb1, 1)
        for jj, last in ((1, 2), (3, 5), (2, 8)):
            @pl.when(t == last)
            def _():
                sbuf[jj - 1] = acc[jj * SLAB : (jj + 1) * SLAB].astype(BF)
                main_send(jj).start()

    for k in range(3):
        pltpu.make_async_copy(skel.at[pl.ds(0, PIECE)], skel.at[pl.ds(0, PIECE)], skr.at[k]).wait()
    basis = interp_basis(skel[...], ranks[block_leaf(0)].astype(F32))

    for q in range(16):
        pltpu.make_async_copy(par.at[q], par.at[q], par_sem.at[q]).wait()
    count = jnp.int32(0)
    source = [jnp.int32(-1)] * 8
    for q in range(16):
        mine = owners[q] == y
        source = [jnp.where(jnp.logical_and(mine, count == k), q, source[k]) for k in range(8)]
        count = count + jnp.where(mine, 1, 0)
    for k in range(8):
        placed[0, k] = jnp.where(source[k] >= 0, par[jnp.maximum(source[k], 0)], 0.0)

    for j in range(3):
        pltpu.make_async_copy(rbuf.at[j], rbuf.at[j], rdr.at[j]).wait()
    samples = acc[:SLAB] + (rbuf[0].astype(F32) + rbuf[1].astype(F32)) + rbuf[2].astype(F32)
    interp[...] = dot3(samples, basis, ((1,), (1,)))

    @pl.when(z == y)
    def _():
        for i in range(2):
            for j in range(WAYS):
                for core in range(2):
                    @pl.when(row_target(i, j, core) != me)
                    def _():
                        row_copy(i, j, core).wait_send()

    for copy in col_sends:
        copy.wait_send()
    for half in range(2):
        for i in range(4):
            om_send(i, half).wait_send()
        for i in range(3):
            forward(2 + 2 * i, half).wait_send()
    for j in range(1, WAYS):
        piv_send(j, 0).wait_send()

        @pl.when(has_sibling(x, z, j))
        def _():
            piv_send(j, 1).wait_send()

        main_send(j).wait_send()
    for k in range(3):
        skel_send(k).wait_send()
    for k in range(4):
        for g in range(4):
            if g:
                par_send(k, g).wait_send()
            else:
                @pl.when(par_dev(k) != me)
                def _():
                    par_send(k, g).wait_send()


def body(points, omega, pivots, ranks, owners):
    vmem = pl.BlockSpec(memory_space=pltpu.VMEM)
    smem = pl.BlockSpec(memory_space=pltpu.SMEM)
    dma = pltpu.SemaphoreType.DMA
    interp, placed = pl.pallas_call(
        sweep_kernel,
        name="sweep",
        out_shape=[
            jax.ShapeDtypeStruct((SLAB, RMAX), F32),
            jax.ShapeDtypeStruct((1, 8, 16, S), F32),
        ],
        in_specs=[vmem, pl.BlockSpec(memory_space=pl.ANY), vmem, smem, smem],
        out_specs=[vmem, vmem],
        scratch_shapes=[
            pltpu.VMEM((8, HALF), F32),
            pltpu.VMEM((2, 2, 8, SLAB // 2 + 128), F32),
            pltpu.VMEM((4, 8, SLAB // 2 + 128), F32),
            pltpu.VMEM((8, 8, HALF), F32),
            pltpu.VMEM((8, LEAF, S), BF),
            pltpu.VMEM((4 * SLAB, DEPTH), BF),
            pltpu.VMEM((RMAX, DEPTH), BF),
            pltpu.VMEM((8, DEPTH, LEAF), BF),
            pltpu.VMEM((4, 4 * SLAB, 128), F32),
            pltpu.VMEM((8, 8, LEAF), F32),
            pltpu.VMEM((4 * SLAB, S), F32),
            pltpu.VMEM((4, 2, PIECE, S), F32),
            pltpu.VMEM((2 * SLAB, HALF), BF),
            pltpu.VMEM((2 * SLAB, HALF), BF),
            pltpu.VMEM((3, SLAB, S), BF),
            pltpu.VMEM((3, SLAB, S), BF),
            pltpu.VMEM((3, 2, PIECE, S), F32),
            pltpu.VMEM((RMAX, S), F32),
            pltpu.VMEM((PIECE, S), F32),
            pltpu.VMEM((16, 16, S), F32),
            dma, dma((7,)), dma((8,)), dma((16,)), dma((4,)), dma((4, 2)), dma((8, 2)), dma((3, 2)),
            dma((3,)), dma((3,)), dma((3, 2)), dma((3, 2)), dma((3,)), dma((3,)), dma((16,)), dma((16,)),
        ],
        compiler_params=pltpu.CompilerParams(
            collective_id=0, has_side_effects=True, vmem_limit_bytes=56 * 2**20
        ),
    )(points, omega, pivots, ranks, owners)
    return interp, placed


def solution(mesh):
    placed = (P(None, "dev"), P("dev", None), P(), P(), P())
    return jax.shard_map(
        body,
        mesh=mesh,
        in_specs=placed,
        out_specs=(P(("grp", "dev"), None), P("grp", None, "dev", None)),
        check_vma=False,
    )
```
